32 devices in a mesh: dp: 4 (over x, core), fsdp: 8 (over z, y).
Axes of the slice: x: 2, y: 2, z: 4, core: 2. Of those that a mesh axis runs over, the one named last changes fastest.
Arguments:
- inputs: bfloat16 [128, 280, 768], P(('dp', 'fsdp')), may hold values from -6 to 6
- patch_count: int32 [128], P(('dp', 'fsdp')), may hold values from 100 to 240
- cotangent: bfloat16 [128, 280, 768], P(('dp', 'fsdp')), may hold values from -6 to 6
- first_gain: bfloat16 [768], P('fsdp'), may hold values from 0.5 to 1.5
- first_shift: bfloat16 [768], P('fsdp'), may hold values from -1.796875 to 1.796875
- triple_weight: bfloat16 [768, 2304], P('fsdp'), may hold values from -0.21875 to 0.21875
- head_bias: bfloat16 [1536], P('fsdp'), may hold values from -1.796875 to 1.796875
- output_weight: bfloat16 [768, 768], P('fsdp'), may hold values from -0.875 to 0.875
- output_bias: bfloat16 [768], P('fsdp'), may hold values from -1.796875 to 1.796875
- second_gain: bfloat16 [768], P('fsdp'), may hold values from 0.5 to 1.5
- second_shift: bfloat16 [768], P('fsdp'), may hold values from -1.796875 to 1.796875
- expand_weight: bfloat16 [768, 3072], P('fsdp'), may hold values from -0.21875 to 0.21875
- expand_bias: bfloat16 [3072], P('fsdp'), may hold values from -1.796875 to 1.796875
- reduce_weight: bfloat16 [3072, 768], P('fsdp'), may hold values from -0.109375 to 0.109375
- reduce_bias: bfloat16 [768], P('fsdp'), may hold values from -1.796875 to 1.796875
Outputs:
- layer_output: bfloat16 [128, 280, 768], P(('dp', 'fsdp'))
- input_gradient: bfloat16 [128, 280, 768], P(('dp', 'fsdp'))
- first_gain_gradient: float32 [768], P('fsdp')
- first_shift_gradient: float32 [768], P('fsdp')
- triple_gradient: float32 [768, 2304], P('fsdp')
- head_bias_gradient: float32 [1536], P('fsdp')
- output_weight_gradient: float32 [768, 768], P('fsdp')
- output_bias_gradient: float32 [768], P('fsdp')
- second_gain_gradient: float32 [768], P('fsdp')
- second_shift_gradient: float32 [768], P('fsdp')
- expand_weight_gradient: float32 [768, 3072], P('fsdp')
- expand_bias_gradient: float32 [3072], P('fsdp')
- reduce_weight_gradient: float32 [3072, 768], P('fsdp')
- reduce_bias_gradient: float32 [768], P('fsdp')
The draws below stay inside these ranges and needn't reach their ends.
Inputs may be any that keep to these rules, and one draw needn't show every extreme that they name: Rows 40 + patch_count to 279 of a pair are padding.
All inputs are finite; a program needn't handle non-finite values.
Results may differ from the reference program's by a relative error of at most 0.018.
Values may be sent and summed in bfloat16 or wider, within the bound.
A program may use at most 192 MiB of HBM per device.

```python
import jax
import jax.numpy as jnp
from jax import lax

D = 768
HEADS = 12
HEAD_DIM = 64
FF = 3072
TEXT = 40
PATCH = 240
SEQ = 280
PAIRS = 128


def plant(drawn, own_key, least, top_value):
    extent = drawn.shape
    index_at = [jax.random.randint(jax.random.fold_in(own_key, axis), (), 0, extent[axis]) for axis in range(len(extent))]
    drawn = drawn.at[tuple(index_at)].set(least)
    longest = extent.index(max(extent))
    index_at[longest] = (index_at[longest] + 1) % extent[longest]
    return drawn.at[tuple(index_at)].set(top_value)


def block_levels(own_key, shape, cuts, smallest, largest):
    def one(dim, shards_of):
        heights = jax.random.uniform(jax.random.fold_in(jax.random.fold_in(own_key, 6), dim), (shards_of,), jnp.float32, smallest / len(cuts), largest / len(cuts))
        return jnp.repeat(jnp.exp(heights), shape[dim] // shards_of).reshape((-1,) + (1,) * (len(shape) - dim - 1))

    level = one(*cuts[0])
    for cut in cuts[1:]:
        level = level * one(*cut)
    return level


def noise(stream_key, extent, scale, reach, split=(), held_as=jnp.bfloat16):
    factor_of = block_levels(stream_key, extent, split, -0.22, 0.18) if split else 1.0
    entries = jax.random.normal(stream_key, extent, jnp.float32) * scale * factor_of
    return jnp.minimum(jnp.maximum(entries, -reach), reach).astype(held_as)


def setup_inputs(seed: int = 0) -> dict:
    keys = jax.random.split(jax.random.key(seed), 16)
    inputs = noise(keys[0], (PAIRS, SEQ, D), 1.0, 6.0, ((0, 32),))
    patch_count = plant(jax.random.randint(keys[1], (PAIRS,), PATCH * 5 // 12, PATCH + 1), jax.random.fold_in(keys[1], 1), PATCH * 5 // 12, PATCH).astype(jnp.int32)
    cotangent = noise(keys[2], (PAIRS, SEQ, D), 1.0, 6.0, ((0, 32),))
    first_gain = jnp.clip(1.0 + 0.1 * jax.random.normal(keys[3], (D,), jnp.float32), 0.5, 1.5).astype(jnp.bfloat16)
    first_shift = noise(keys[4], (D,), 0.3, 1.796875, ((0, 8),))
    triple_weight = noise(keys[5], (D, 3 * D), D ** -0.5, 0.21875, ((0, 8),))
    head_bias = noise(keys[6], (2 * D,), 0.3, 1.796875, ((0, 8),))
    output_weight = noise(keys[7], (D, D), (D // 16) ** -0.5, 0.875, ((0, 8),))
    output_bias = noise(keys[8], (D,), 0.3, 1.796875, ((0, 8),))
    second_gain = jnp.clip(1.0 + 0.1 * jax.random.normal(keys[9], (D,), jnp.float32), 0.5, 1.5).astype(jnp.bfloat16)
    second_shift = noise(keys[10], (D,), 0.3, 1.796875, ((0, 8),))
    expand_weight = noise(keys[11], (D, FF), D ** -0.5, 0.21875, ((0, 8),))
    expand_bias = noise(keys[12], (FF,), 0.3, 1.796875, ((0, 8),))
    reduce_weight = noise(keys[13], (FF, D), FF ** -0.5, 0.109375, ((0, 8),))
    reduce_bias = noise(keys[14], (D,), 0.3, 1.796875, ((0, 8),))
    return {"inputs": inputs, "patch_count": patch_count, "cotangent": cotangent, "first_gain": first_gain, "first_shift": first_shift, "triple_weight": triple_weight, "head_bias": head_bias, "output_weight": output_weight, "output_bias": output_bias, "second_gain": second_gain, "second_shift": second_shift, "expand_weight": expand_weight, "expand_bias": expand_bias, "reduce_weight": reduce_weight, "reduce_bias": reduce_bias}


NORM_EPSILON = 1e-06

@jax.custom_vjp
def low(v):
    return lax.optimization_barrier(v.astype(jnp.bfloat16)).astype(jnp.float32)

@jax.custom_vjp
def low_back(v):
    return v

def low_keep(v):
    return (low(v), None)

def low_pass(kept, grad):
    return (grad,)

def back_keep(v):
    return (v, None)

def back_low(kept, grad):
    return (low(grad),)
low.defvjp(low_keep, low_pass)
low_back.defvjp(back_keep, back_low)

def matmul(left, right):
    return jnp.einsum('gsd,de->gse', left, right, precision=lax.Precision.HIGHEST)

def layer_norm(values, gain, shift):
    centred = values - lax.optimization_barrier(jnp.mean(values, axis=-1, keepdims=True))
    variance = lax.optimization_barrier(jnp.mean(centred * centred, axis=-1, keepdims=True))
    return centred * lax.rsqrt(variance + NORM_EPSILON) * gain + shift

def forward(values, valid_rows, params):
    gain_one, shift_one, triple, biases, project, project_bias, gain_two, shift_two, expand, expand_add, shrink, shrink_add = params
    groups, length, width = values.shape
    hidden_one = low(layer_norm(values, gain_one, shift_one))
    bias_row = jnp.concatenate([biases[:width], jnp.zeros((width,), jnp.float32), biases[width:]])
    triple_rows = low(low_back(matmul(hidden_one, triple) + bias_row))
    query_rows = triple_rows[..., :width].reshape(groups, length, HEADS, HEAD_DIM)
    key_rows = triple_rows[..., width:2 * width].reshape(groups, length, HEADS, HEAD_DIM)
    value_rows = triple_rows[..., 2 * width:].reshape(groups, length, HEADS, HEAD_DIM)
    score_scale = HEAD_DIM ** (-0.5)
    scores = low_back(jnp.einsum('gshd,gthd->ghst', query_rows, key_rows, precision=lax.Precision.HIGHEST) * score_scale)
    scores = jnp.where(valid_rows[:, None, None, :] > 0, scores, -1e+30)
    probs = low(jax.nn.softmax(scores, axis=-1))
    context = jnp.einsum('ghst,gthd->gshd', probs, value_rows, precision=lax.Precision.HIGHEST).reshape(groups, length, width)
    context = low(low_back(context))
    branch = low_back(matmul(context, project) + project_bias)
    middle = values + branch
    hidden_two = low(layer_norm(middle, gain_two, shift_two))
    pre_act = low_back(matmul(hidden_two, expand) + expand_add)
    activated = low(jax.nn.gelu(pre_act, approximate=False))
    mixed = low_back(matmul(activated, shrink) + shrink_add)
    return valid_rows[..., None] * (middle + mixed)

def reference(inputs, patch_count, cotangent, first_gain, first_shift, triple_weight, head_bias, output_weight, output_bias, second_gain, second_shift, expand_weight, expand_bias, reduce_weight, reduce_bias):
    params = tuple((item.astype(jnp.float32) for item in (first_gain, first_shift, triple_weight, head_bias, output_weight, output_bias, second_gain, second_shift, expand_weight, expand_bias, reduce_weight, reduce_bias)))
    positions = jnp.arange(SEQ, dtype=jnp.int32)
    valid_rows = (positions[None, :] < TEXT + patch_count[:, None]).astype(jnp.float32)
    group_pairs = 8
    count_groups = PAIRS // group_pairs
    stacked_inputs = inputs.reshape(count_groups, group_pairs, SEQ, D)
    stacked_valid = valid_rows.reshape(count_groups, group_pairs, SEQ)
    stacked_cot = cotangent.reshape(count_groups, group_pairs, SEQ, D)
    zeros_tree = tuple((jnp.zeros_like(item) for item in params))

    def group_step(totals, member):
        values_in, valid_in, cot_in = member
        outputs, pullback = jax.vjp(lambda values, weights: forward(values, valid_in, weights), values_in.astype(jnp.float32), params)
        input_grad, weight_grads = pullback(cot_in.astype(jnp.float32))
        totals = tuple((first + second for first, second in zip(totals, weight_grads)))
        return (totals, (outputs.astype(jnp.bfloat16), input_grad.astype(jnp.bfloat16)))
    totals, (outputs, input_grads) = lax.scan(group_step, zeros_tree, (stacked_inputs, stacked_valid, stacked_cot))
    layer_output = outputs.reshape(PAIRS, SEQ, D)
    input_gradient = input_grads.reshape(PAIRS, SEQ, D)
    return (layer_output, input_gradient, totals[0], totals[1], totals[2], totals[3], totals[4], totals[5], totals[6], totals[7], totals[8], totals[9], totals[10], totals[11])
```

```python
import functools

import jax
import jax.numpy as jnp
from jax import lax
from jax.experimental import pallas as pl
from jax.experimental.pallas import tpu as pltpu
from jax.sharding import PartitionSpec as P

HEADS = 12
HEAD_DIM = 64
TEXT = 40
MESH = pl.DeviceIdType.MESH


class Grid:
    def __init__(self, fsdp, dp):
        self.H = dp // 4
        y_size = 1
        while y_size * y_size * 8 <= fsdp:
            y_size *= 2
        self.F, self.Y, self.Z = fsdp, y_size, fsdp // y_size

    def locate(self):
        self.dp = lax.axis_index("dp")
        self.f = lax.axis_index("fsdp")
        self.c = lax.rem(self.dp, 2)
        self.x = lax.rem(self.dp // 2, 2)
        self.h = self.dp // 4
        self.z = self.f // self.Y
        self.y = lax.rem(self.f, self.Y)
        return self

    def core_peer(self):
        return (self.dp + 1 - 2 * self.c, self.f)

    def x_peer(self):
        return (self.dp + 2 - 4 * self.x, self.f)

    def far_index(self, dh):
        return lax.rem(self.h + self.H + dh, self.H)

    def far_peer(self, dh):
        return (self.far_index(dh) * 4 + lax.rem(self.dp, 4), self.f)

    def z_index(self, dz):
        return lax.rem(self.z + self.Z + dz, self.Z)

    def y_index(self, dy):
        return lax.rem(self.y + self.Y + dy, self.Y)

    def z_peer(self, dz):
        return (self.dp, self.z_index(dz) * self.Y + self.y)

    def y_peer(self, dy):
        return (self.dp, self.z * self.Y + self.y_index(dy))

    def source(self, dz, dy):
        return self.z_index(-dz) * self.Y + self.y_index(-dy)

    def greet(self):
        barrier = pltpu.get_barrier_semaphore()
        peers = [self.core_peer(), self.x_peer()]
        peers += [self.z_peer(dz) for dz in range(1, self.Z)]
        peers += [self.y_peer(dy) for dy in range(1, self.Y)]
        peers += [self.far_peer(dh) for dh in range(1, self.H)]
        for peer in peers:
            pl.semaphore_signal(barrier, inc=1, device_id=peer, device_id_type=MESH)
        pl.semaphore_wait(barrier, len(peers))


def remote(src, dst, send, recv, peer):
    return pltpu.make_async_remote_copy(
        src_ref=src,
        dst_ref=dst,
        send_sem=send,
        recv_sem=recv,
        device_id=peer,
        device_id_type=MESH,
    )


def lanes(start, width):
    return pl.ds(pl.multiple_of(start, 128), width)


class Gather:
    def __init__(self, grid, src, dst, rows, col, width, send, recv):
        self.g, self.src, self.dst, self.rows = grid, src, dst, rows
        self.send, self.recv = send, recv
        self.half, self.group = width // 2, width // 6
        self.col = col
        self.sent = []
        g = grid
        self.mine = lanes(col + g.c * self.half + g.x * self.group, 2 * self.group)
        self.x_out = lanes(col + g.c * self.half + 2 * g.x * self.group, self.group)
        self.x_in = lanes(col + g.c * self.half + 2 * (1 - g.x) * self.group, self.group)
        self.core_out = lanes(col + g.c * self.half, self.half)
        self.core_in = lanes(col + (1 - g.c) * self.half, self.half)
        self.z_base, self.y_base = 0, g.Z - 1
        self.x_base = self.y_base + g.Z * (g.Y - 1)
        self.c_base = self.x_base + g.F - 1

    @staticmethod
    def count(grid):
        return grid.Z - 1 + grid.Z * (grid.Y - 1) + 2 * (grid.F - 1)

    def view(self, shard, columns):
        return self.dst.at[shard, self.rows, columns]

    def push(self, src, dst, index, peer):
        copy = remote(src, dst, self.send.at[index], self.recv.at[index], peer)
        copy.start()
        self.sent.append(copy)

    def arrive(self, view, index):
        pltpu.make_async_copy(view, view, self.recv.at[index]).wait()

    def pairs(self):
        return [(dz, dy) for dy in range(self.g.Y) for dz in range(self.g.Z) if dz + dy > 0]

    def slot(self, dz, dy):
        return dz * self.g.Y + dy - 1

    def begin(self):
        g = self.g
        own = self.src.at[self.rows, self.mine]
        for dz in range(1, g.Z):
            self.push(own, self.view(g.f, self.mine), self.z_base + dz - 1, g.z_peer(dz))
        for dy in range(1, g.Y):
            self.push(own, self.view(g.f, self.mine), self.y_base + dy - 1, g.y_peer(dy))

    def over_y(self):
        g = self.g
        for dz in range(1, g.Z):
            shard = g.source(dz, 0)
            self.arrive(self.view(shard, self.mine), self.z_base + dz - 1)
            for dy in range(1, g.Y):
                self.push(
                    self.view(shard, self.mine),
                    self.view(shard, self.mine),
                    self.y_base + dz * (g.Y - 1) + dy - 1,
                    g.y_peer(dy),
                )
            self.over_x(dz, 0)

    def over_x(self, dz, dy):
        g = self.g
        shard = g.source(dz, dy)
        self.push(
            self.view(shard, self.x_out),
            self.view(shard, self.x_out),
            self.x_base + self.slot(dz, dy),
            g.x_peer(),
        )

    def finish_y(self):
        g = self.g
        for dz in range(g.Z):
            for dy in range(1, g.Y):
                shard = g.source(dz, dy)
                self.arrive(self.view(shard, self.mine), self.y_base + dz * (g.Y - 1) + dy - 1)
                self.over_x(dz, dy)

    def over_core(self):
        g = self.g
        for dz, dy in self.pairs():
            shard = g.source(dz, dy)
            self.arrive(self.view(shard, self.x_in), self.x_base + self.slot(dz, dy))
            self.push(
                self.view(shard, self.core_out),
                self.view(shard, self.core_out),
                self.c_base + self.slot(dz, dy),
                g.core_peer(),
            )

    def finish(self):
        g = self.g
        for dz, dy in self.pairs():
            shard = g.source(dz, dy)
            self.arrive(self.view(shard, self.core_in), self.c_base + self.slot(dz, dy))

    def drain(self):
        for copy in self.sent:
            copy.wait_send()


def gather_kernel(grid, pieces, *refs):
    n = len(pieces)
    count = refs_count(pieces)
    sources, outs = refs[:count], refs[count : 2 * count]
    send, recv, local = refs[2 * count :]
    grid.locate()
    owns = []
    for index in range(count):
        own = pltpu.make_async_copy(sources[index], outs[index].at[grid.f], local.at[index])
        own.start()
        owns.append(own)
    grid.greet()
    chunks = [
        Gather(grid, sources[which], outs[which], pl.ds(row, rows), col, width, send.at[i], recv.at[i])
        for i, (which, row, rows, col, width) in enumerate(pieces)
    ]
    for chunk in chunks:
        chunk.begin()
    for step in range(n + 2):
        if step < n:
            chunks[step].over_y()
        if 0 <= step - 1 < n:
            chunks[step - 1].finish_y()
        if 0 <= step - 2 < n:
            chunks[step - 2].over_core()
    for chunk in chunks:
        chunk.finish()
    for chunk in chunks:
        chunk.drain()
    for own in owns:
        own.wait()


def refs_count(pieces):
    return 1 + max(piece[0] for piece in pieces)


def gather_all(fsdp, dp, arrays):
    grid = Grid(fsdp, dp)
    pieces = []
    for which, array in enumerate(arrays):
        rows, width = array.shape
        if rows * width < 96 * 3072 * 96 // fsdp // 12 // 8 * 8 or which < 3:
            pieces.append((which, 0, rows, 0, width))
        elif width > 1536:
            pieces.append((which, 0, rows, 0, width // 2))
            pieces.append((which, 0, rows, width // 2, width // 2))
        else:
            pieces.append((which, 0, rows // 2, 0, width))
            pieces.append((which, rows // 2, rows // 2, 0, width))
    count = Gather.count(grid)
    hbm = pl.BlockSpec(memory_space=pltpu.HBM)
    return pl.pallas_call(
        functools.partial(gather_kernel, grid, pieces),
        out_shape=[jax.ShapeDtypeStruct((fsdp,) + a.shape, a.dtype) for a in arrays],
        in_specs=[hbm] * len(arrays),
        out_specs=[hbm] * len(arrays),
        scratch_shapes=[
            pltpu.SemaphoreType.DMA((len(pieces), count)),
            pltpu.SemaphoreType.DMA((len(pieces), count)),
            pltpu.SemaphoreType.DMA((len(arrays),)),
        ],
        compiler_params=pltpu.CompilerParams(collective_id=0, has_side_effects=True),
        name="gather_weights",
    )(*arrays)


class Scatter:
    def __init__(self, grid, src, out, rows, col, width, apart, bufs, send, recv, local):
        g = self.g = grid
        self.src, self.out, self.rows = src, out, rows
        self.send, self.recv, self.local = send, recv, local
        self.half, self.apart = width // 2, apart
        self.shared = self.half - 2 * apart
        self.core_keep = lanes(col + g.c * self.half, self.half)
        self.core_give = lanes(col + (1 - g.c) * self.half, self.half)
        self.x_keep = lanes(g.x * (apart + self.shared), apart)
        self.x_give = lanes((1 - g.x) * (apart + self.shared), apart)
        self.kept = lanes(g.x * apart, apart + self.shared)
        self.out_keep, self.out_give = self.core_keep, self.core_give
        self.near, self.core_in, self.x_in, self.y_in, self.z_sum, self.z_in, self.f_out, self.f_in, self.e_out, self.far = bufs
        self.sent = []

    @staticmethod
    def buffers(grid, rows, width, apart):
        half = width // 2
        part = half - apart
        bf = jnp.bfloat16
        return [
            pltpu.VMEM((grid.F, rows, half), bf),
            pltpu.VMEM((grid.F, rows, half), bf),
            pltpu.VMEM((grid.F, rows, apart), bf),
            pltpu.VMEM((grid.Y, grid.Z, rows, part), bf),
            pltpu.VMEM((grid.Z, rows, part), bf),
            pltpu.VMEM((grid.Z, rows, part), bf),
            pltpu.VMEM((rows, part), bf),
            pltpu.VMEM((rows, part), bf),
            pltpu.VMEM((2, rows, half), bf),
            pltpu.VMEM((grid.H, rows, part), bf),
        ]

    @staticmethod
    def count(grid):
        return 4 + grid.Z * (grid.Y - 1) + grid.Z - 1 + grid.H - 1

    def push(self, src, dst, index, peer):
        copy = remote(src, dst, self.send.at[index], self.recv.at[index], peer)
        copy.start()
        self.sent.append(copy)

    def arrive(self, view, index):
        pltpu.make_async_copy(view, view, self.recv.at[index]).wait()

    def begin(self):
        self.own = pltpu.make_async_copy(self.src.at[:, self.rows, self.core_keep], self.near, self.local)
        self.own.start()
        self.push(self.src.at[:, self.rows, self.core_give], self.core_in, 0, self.g.core_peer())

    def add(self, count, body):
        def step(i, carry):
            body(i)
            return carry

        lax.fori_loop(0, count, step, 0)

    def over_x(self):
        self.own.wait()
        self.arrive(self.core_in, 0)

        def body(i):
            self.near[i] = plus(self.near[i], self.core_in[i])

        self.add(self.g.F, body)
        self.push(self.near.at[:, :, self.x_give], self.x_in, 1, self.g.x_peer())

    def over_y(self):
        g = self.g
        self.arrive(self.x_in, 1)

        def body(i):
            self.near[i, :, self.x_keep] = plus(self.near[i, :, self.x_keep], self.x_in[i])

        self.add(g.F, body)
        for dz in range(g.Z):
            for dy in range(1, g.Y):
                self.push(
                    self.near.at[dz * g.Y + g.y_index(dy), :, self.kept],
                    self.y_in.at[dy, dz],
                    4 + dz * (g.Y - 1) + dy - 1,
                    g.y_peer(dy),
                )

    def over_z(self):
        g = self.g
        for dz in range(g.Z):
            for dy in range(1, g.Y):
                self.arrive(self.y_in.at[dy, dz], 4 + dz * (g.Y - 1) + dy - 1)

        def body(i):
            total = self.near[i * g.Y + g.y, :, self.kept].astype(jnp.float32)
            for dy in range(1, g.Y):
                total += self.y_in[dy, i].astype(jnp.float32)
            self.z_sum[i] = total.astype(jnp.bfloat16)

        self.add(g.Z, body)
        for dz in range(1, g.Z):
            self.push(
                self.z_sum.at[g.z_index(dz)],
                self.z_in.at[dz],
                4 + g.Z * (g.Y - 1) + dz - 1,
                g.z_peer(dz),
            )

    def over_pair(self):
        g = self.g
        for dz in range(1, g.Z):
            self.arrive(self.z_in.at[dz], 4 + g.Z * (g.Y - 1) + dz - 1)
        total = self.z_sum[g.z].astype(jnp.float32)
        for dz in range(1, g.Z):
            total += self.z_in[dz].astype(jnp.float32)
        self.f_out[...] = total.astype(jnp.bfloat16)
        if g.H > 1:
            self.over_far()
        self.push(self.f_out, self.f_in, 2, g.x_peer())

    def over_far(self):
        g = self.g
        base = 4 + g.Z * (g.Y - 1) + g.Z - 2
        self.far[g.h] = self.f_out[...]
        for dh in range(1, g.H):
            self.push(self.f_out, self.far.at[g.h], base + dh, g.far_peer(dh))
        for dh in range(1, g.H):
            self.arrive(self.far.at[g.far_index(-dh)], base + dh)
        for copy in self.sent[1 - g.H :]:
            copy.wait_send()
        del self.sent[1 - g.H :]
        total = self.far[0].astype(jnp.float32)
        for h in range(1, g.H):
            total += self.far[h].astype(jnp.float32)
        self.f_out[...] = total.astype(jnp.bfloat16)

    def over_core(self):
        g = self.g
        self.arrive(self.f_in, 2)
        shared_out = lanes((1 - g.x) * self.apart, self.shared)
        shared_in = lanes(g.x * self.apart, self.shared)
        own = lanes(g.x * self.shared, self.apart)
        other = lanes((1 - g.x) * self.shared, self.apart)
        e = self.e_out.at[0]
        e[:, lanes(self.apart, self.shared)] = plus(self.f_out[:, shared_out], self.f_in[:, shared_in])
        e[:, self.x_keep] = self.f_out[:, own]
        e[:, self.x_give] = self.f_in[:, other]
        self.push(e, self.e_out.at[1], 3, g.core_peer())

    def finish(self):
        self.arrive(self.e_out.at[1], 3)
        self.out[self.rows, self.out_keep] = self.e_out[0].astype(jnp.float32)
        self.out[self.rows, self.out_give] = self.e_out[1].astype(jnp.float32)

    def drain(self):
        for copy in self.sent:
            copy.wait_send()


def plus(left, right):
    return (left.astype(jnp.float32) + right.astype(jnp.float32)).astype(jnp.bfloat16)


def scatter_kernel(grid, pieces, *refs):
    n = len(pieces)
    count = refs_count(pieces)
    sources, outs = refs[:count], refs[count : 2 * count]
    bufs = refs[2 * count : 2 * count + 10 * n]
    send, recv, local = refs[2 * count + 10 * n :]
    grid.locate()
    grid.greet()
    chunks = [
        Scatter(
            grid,
            sources[which],
            outs[which],
            pl.ds(row, rows),
            col,
            width,
            apart,
            bufs[10 * i : 10 * i + 10],
            send.at[i],
            recv.at[i],
            local.at[i],
        )
        for i, (which, row, rows, col, width, apart) in enumerate(pieces)
    ]
    for chunk in chunks:
        chunk.begin()
    stages = ["over_x", "over_y", "over_z", "over_pair", "over_core", "finish"]
    for step in range(n + len(stages) - 1):
        for depth, stage in enumerate(stages):
            if 0 <= step - depth < n:
                getattr(chunks[step - depth], stage)()
    for chunk in chunks:
        chunk.drain()


def scatter_all(fsdp, dp, arrays):
    grid = Grid(fsdp, dp)
    pieces = []
    for which, array in enumerate(arrays):
        rows, width = array.shape[1:]
        if width == 3072:
            pieces += [(which, 0, rows, col, 1536, 128) for col in (0, 1536)]
        elif width == 2304:
            pieces += [(which, 0, rows, 0, 1536, 128), (which, 0, rows, 1536, 768, 128)]
        elif rows * fsdp > 768:
            pieces += [(which, row, rows // 2, 0, width, 128) for row in (0, rows // 2)]
        else:
            pieces.append((which, 0, rows, 0, width, 128))
    count = Scatter.count(grid)
    hbm = pl.BlockSpec(memory_space=pltpu.HBM)
    vmem = pl.BlockSpec(memory_space=pltpu.VMEM)
    scratch = []
    for _, _, rows, _, width, apart in pieces:
        scratch += Scatter.buffers(grid, rows, width, apart)
    return pl.pallas_call(
        functools.partial(scatter_kernel, grid, pieces),
        out_shape=[jax.ShapeDtypeStruct(a.shape[1:], jnp.float32) for a in arrays],
        in_specs=[hbm] * len(arrays),
        out_specs=[vmem] * len(arrays),
        scratch_shapes=scratch
        + [
            pltpu.SemaphoreType.DMA((len(pieces), count)),
            pltpu.SemaphoreType.DMA((len(pieces), count)),
            pltpu.SemaphoreType.DMA((len(pieces),)),
        ],
        compiler_params=pltpu.CompilerParams(
            collective_id=1, has_side_effects=True, vmem_limit_bytes=56 * 1024 * 1024
        ),
        name="scatter_gradients",
    )(*arrays)


NORM_EPSILON = 1e-06


def layer_norm(values, gain, shift):
    centred = values - jnp.mean(values, axis=-1, keepdims=True)
    variance = jnp.mean(centred * centred, axis=-1, keepdims=True)
    return centred * lax.rsqrt(variance + NORM_EPSILON) * gain + shift


def project_rows(left, right):
    return jnp.einsum("psd,de->pse", left, right, preferred_element_type=jnp.float32)


def back_rows(left, right):
    return jnp.einsum("pse,de->psd", left, right, preferred_element_type=jnp.float32)


def outer_rows(left, right):
    return jnp.einsum("psd,pse->de", left, right, preferred_element_type=jnp.float32)


def row_total(values):
    return jnp.sum(values.astype(jnp.float32), axis=(0, 1))


def shards(
    inputs,
    patch_count,
    cotangent,
    first_gain,
    first_shift,
    triple_weight,
    head_bias,
    output_weight,
    output_bias,
    second_gain,
    second_shift,
    expand_weight,
    expand_bias,
    reduce_weight,
    reduce_bias,
):
    fsdp, dp = lax.axis_size("fsdp"), lax.axis_size("dp")
    small = (
        first_gain,
        first_shift,
        head_bias,
        output_bias,
        second_gain,
        second_shift,
        expand_bias,
        reduce_bias,
    )
    packed = jnp.stack([jnp.pad(item, (0, 768 - item.shape[0])) for item in small])
    packed, triple, project, expand, shrink = gather_all(
        fsdp, dp, (packed, triple_weight, output_weight, expand_weight, reduce_weight)
    )
    gain_one, shift_one, biases, project_bias, gain_two, shift_two, expand_add, shrink_add = (
        packed[:, index, : item.shape[0]].reshape(-1) for index, item in enumerate(small)
    )
    triple = triple.reshape(-1, triple.shape[-1])
    project = project.reshape(-1, project.shape[-1])
    expand = expand.reshape(-1, expand.shape[-1])
    shrink = shrink.reshape(-1, shrink.shape[-1])
    pairs, length, width = inputs.shape
    positions = lax.broadcasted_iota(jnp.int32, (pairs, length), 1)
    valid_rows = (positions < TEXT + patch_count[:, None]).astype(jnp.float32)
    key_mask = valid_rows[:, None, None, :] > 0
    score_scale = HEAD_DIM ** (-0.5)
    inputs_wide = inputs.astype(jnp.float32)
    hidden_one = layer_norm(
        inputs_wide, gain_one.astype(jnp.float32), shift_one.astype(jnp.float32)
    ).astype(jnp.bfloat16)
    biases_wide = biases.astype(jnp.float32)
    bias_row = jnp.concatenate(
        [biases_wide[:width], jnp.zeros((width,), jnp.float32), biases_wide[width:]]
    )
    triple_rows = (project_rows(hidden_one, triple) + bias_row).astype(jnp.bfloat16)
    query_rows = triple_rows[..., :width].reshape(pairs, length, HEADS, HEAD_DIM)
    key_rows = triple_rows[..., width : 2 * width].reshape(pairs, length, HEADS, HEAD_DIM)
    value_rows = triple_rows[..., 2 * width :].reshape(pairs, length, HEADS, HEAD_DIM)

    def scores_of(queries_in, keys_in):
        raw_scores = (
            jnp.einsum("pshd,pthd->phst", queries_in, keys_in, preferred_element_type=jnp.float32)
            * score_scale
        )
        return jnp.where(key_mask, raw_scores, -1e30)

    scores = scores_of(query_rows, key_rows)
    row_max = jnp.max(scores, axis=-1, keepdims=True)
    expo = jnp.exp(scores - row_max)
    expo_total = jnp.sum(expo, axis=-1, keepdims=True)
    probs = expo / expo_total
    row_lse = row_max + jnp.log(expo_total)
    context = jnp.einsum(
        "phst,pthd->pshd",
        probs.astype(jnp.bfloat16),
        value_rows,
        preferred_element_type=jnp.float32,
    )
    context = context.reshape(pairs, length, width).astype(jnp.bfloat16)
    middle = inputs_wide + project_rows(context, project) + project_bias.astype(jnp.float32)
    hidden_two = layer_norm(
        middle, gain_two.astype(jnp.float32), shift_two.astype(jnp.float32)
    ).astype(jnp.bfloat16)
    pre_act = project_rows(hidden_two, expand) + expand_add.astype(jnp.float32)
    activated = jax.nn.gelu(pre_act, approximate=False).astype(jnp.bfloat16)
    mixed = project_rows(activated, shrink) + shrink_add.astype(jnp.float32)
    layer_output = (valid_rows[..., None] * (middle + mixed)).astype(jnp.bfloat16)
    gain_one_back, triple_back, project_back = gain_one, triple, project
    gain_two_back, expand_back, shrink_back = gain_two, expand, shrink
    upstream = cotangent.astype(jnp.float32) * valid_rows[..., None]
    upstream_low = upstream.astype(jnp.bfloat16)
    shrink_add_grad = row_total(upstream_low)
    shrink_grad = outer_rows(activated, upstream_low)
    act_grad = back_rows(upstream_low, shrink_back)
    gelu_value, gelu_back = jax.vjp(lambda entry: jax.nn.gelu(entry, approximate=False), pre_act)
    pre_grad = gelu_back(act_grad)[0].astype(jnp.bfloat16)
    expand_add_grad = row_total(pre_grad)
    expand_grad = outer_rows(hidden_two, pre_grad)
    hidden_two_grad = back_rows(pre_grad, expand_back)
    zero_shift = jnp.zeros((width,), jnp.float32)
    norm_value, norm_back_two = jax.vjp(
        layer_norm, middle, gain_two_back.astype(jnp.float32), zero_shift
    )
    middle_part, gain_two_grad, shift_two_grad = norm_back_two(hidden_two_grad)
    middle_grad = upstream + middle_part
    branch_low = middle_grad.astype(jnp.bfloat16)
    project_bias_grad = row_total(branch_low)
    project_grad = outer_rows(context, branch_low)
    context_grad = (
        back_rows(branch_low, project_back)
        .astype(jnp.bfloat16)
        .reshape(pairs, length, HEADS, HEAD_DIM)
    )
    probs_again = jnp.exp(scores_of(query_rows, key_rows) - row_lse)
    value_grad = jnp.einsum(
        "phst,pshd->pthd",
        probs_again.astype(jnp.bfloat16),
        context_grad,
        preferred_element_type=jnp.float32,
    )
    probs_grad = jnp.einsum(
        "pshd,pthd->phst", context_grad, value_rows, preferred_element_type=jnp.float32
    )
    score_grad = (
        probs_again * (probs_grad - jnp.sum(probs_again * probs_grad, axis=-1, keepdims=True))
    ).astype(jnp.bfloat16)
    query_grad = (
        jnp.einsum("phst,pthd->pshd", score_grad, key_rows, preferred_element_type=jnp.float32)
        * score_scale
    )
    key_grad = (
        jnp.einsum("phst,pshd->pthd", score_grad, query_rows, preferred_element_type=jnp.float32)
        * score_scale
    )
    triple_grad_rows = jnp.concatenate(
        [
            query_grad.reshape(pairs, length, width),
            key_grad.reshape(pairs, length, width),
            value_grad.reshape(pairs, length, width),
        ],
        axis=-1,
    ).astype(jnp.bfloat16)
    bias_sums = row_total(triple_grad_rows)
    head_bias_grad = jnp.concatenate([bias_sums[:width], bias_sums[2 * width :]])
    triple_grad = outer_rows(hidden_one, triple_grad_rows)
    hidden_one_grad = back_rows(triple_grad_rows, triple_back)
    norm_again, norm_back_one = jax.vjp(
        layer_norm, inputs_wide, gain_one_back.astype(jnp.float32), zero_shift
    )
    input_part, gain_one_grad, shift_one_grad = norm_back_one(hidden_one_grad)
    input_gradient = (middle_grad + input_part).astype(jnp.bfloat16)
    small_grads = (
        gain_one_grad,
        shift_one_grad,
        head_bias_grad,
        project_bias_grad,
        gain_two_grad,
        shift_two_grad,
        expand_add_grad,
        shrink_add_grad,
    )
    packed_grad = jnp.stack(
        [
            jnp.pad(
                item.astype(jnp.bfloat16).reshape(fsdp, -1),
                ((0, 0), (0, 768 - item.shape[0] // fsdp)),
            )
            for item in small_grads
        ],
        axis=1,
    )
    shares = scatter_all(
        fsdp,
        dp,
        tuple(
            item.astype(jnp.bfloat16).reshape(fsdp, -1, item.shape[-1])
            for item in (shrink_grad, expand_grad, project_grad, triple_grad)
        )
        + (packed_grad,),
    )
    (
        gain_one_sum,
        shift_one_sum,
        head_bias_sum,
        project_bias_sum,
        gain_two_sum,
        shift_two_sum,
        expand_add_sum,
        shrink_add_sum,
    ) = (shares[4][index, : item.shape[0] // fsdp] for index, item in enumerate(small_grads))
    return (
        layer_output,
        input_gradient,
        gain_one_sum,
        shift_one_sum,
        shares[3],
        head_bias_sum,
        shares[2],
        project_bias_sum,
        gain_two_sum,
        shift_two_sum,
        shares[1],
        expand_add_sum,
        shares[0],
        shrink_add_sum,
    )


def solution(mesh):
    in_specs = (
        P(("dp", "fsdp"), None, None),
        P(("dp", "fsdp")),
        P(("dp", "fsdp"), None, None),
        P("fsdp"),
        P("fsdp"),
        P("fsdp", None),
        P("fsdp"),
        P("fsdp", None),
        P("fsdp"),
        P("fsdp"),
        P("fsdp"),
        P("fsdp", None),
        P("fsdp"),
        P("fsdp", None),
        P("fsdp"),
    )
    out_specs = (
        P(("dp", "fsdp"), None, None),
        P(("dp", "fsdp"), None, None),
        P("fsdp"),
        P("fsdp"),
        P("fsdp", None),
        P("fsdp"),
        P("fsdp", None),
        P("fsdp"),
        P("fsdp"),
        P("fsdp"),
        P("fsdp", None),
        P("fsdp"),
        P("fsdp", None),
        P("fsdp"),
    )
    return jax.shard_map(shards, mesh=mesh, in_specs=in_specs, out_specs=out_specs, check_vma=False)
```

```python
import functools

import jax
import jax.numpy as jnp
from jax import lax
from jax.experimental import pallas as pl
from jax.experimental.pallas import tpu as pltpu
from jax.sharding import PartitionSpec as P

HEADS = 12
HEAD_DIM = 64
TEXT = 40
MESH = pl.DeviceIdType.MESH


class Grid:
    def __init__(self, fsdp, dp):
        self.H = dp // 4
        y_size = 1
        while y_size * y_size * 8 <= fsdp:
            y_size *= 2
        self.F, self.Y, self.Z = fsdp, y_size, fsdp // y_size

    def locate(self):
        self.dp = lax.axis_index("dp")
        self.f = lax.axis_index("fsdp")
        self.c = lax.rem(self.dp, 2)
        self.x = lax.rem(self.dp // 2, 2)
        self.h = self.dp // 4
        self.z = self.f // self.Y
        self.y = lax.rem(self.f, self.Y)
        return self

    def core_peer(self):
        return (self.dp + 1 - 2 * self.c, self.f)

    def x_peer(self):
        return (self.dp + 2 - 4 * self.x, self.f)

    def far_index(self, dh):
        return lax.rem(self.h + self.H + dh, self.H)

    def far_peer(self, dh):
        return (self.far_index(dh) * 4 + lax.rem(self.dp, 4), self.f)

    def z_index(self, dz):
        return lax.rem(self.z + self.Z + dz, self.Z)

    def y_index(self, dy):
        return lax.rem(self.y + self.Y + dy, self.Y)

    def z_peer(self, dz):
        return (self.dp, self.z_index(dz) * self.Y + self.y)

    def y_peer(self, dy):
        return (self.dp, self.z * self.Y + self.y_index(dy))

    def source(self, dz, dy):
        return self.z_index(-dz) * self.Y + self.y_index(-dy)

    def greet(self):
        barrier = pltpu.get_barrier_semaphore()
        peers = [self.core_peer(), self.x_peer()]
        peers += [self.z_peer(dz) for dz in range(1, self.Z)]
        peers += [self.y_peer(dy) for dy in range(1, self.Y)]
        peers += [self.far_peer(dh) for dh in range(1, self.H)]
        for peer in peers:
            pl.semaphore_signal(barrier, inc=1, device_id=peer, device_id_type=MESH)
        pl.semaphore_wait(barrier, len(peers))


def remote(src, dst, send, recv, peer):
    return pltpu.make_async_remote_copy(
        src_ref=src,
        dst_ref=dst,
        send_sem=send,
        recv_sem=recv,
        device_id=peer,
        device_id_type=MESH,
    )


def lanes(start, width):
    return pl.ds(pl.multiple_of(start, 128), width)


class Gather:
    def __init__(self, grid, src, dst, depth, row, rows, col, width, send, recv):
        self.g, self.src, self.dst = grid, src, dst
        self.depth, self.row, self.rows = depth, row, rows
        self.send, self.recv = send, recv
        half, group = width // 2, width // 6
        self.sent = []
        g = grid
        self.mine = lanes(col + g.c * half + g.x * group, 2 * group)
        self.x_out = lanes(col + g.c * half + 2 * g.x * group, group)
        self.x_in = lanes(col + g.c * half + 2 * (1 - g.x) * group, group)
        self.core_out = lanes(col + g.c * half, half)
        self.core_in = lanes(col + (1 - g.c) * half, half)
        self.z_base, self.y_base = 0, g.Z - 1
        self.x_base = self.y_base + g.Z * (g.Y - 1)
        self.c_base = self.x_base + g.F - 1

    @staticmethod
    def count(grid):
        return grid.Z - 1 + grid.Z * (grid.Y - 1) + 2 * (grid.F - 1)

    def view(self, shard, columns):
        start = pl.multiple_of(shard * self.depth + self.row, 8)
        return self.dst.at[pl.ds(start, self.rows), columns]

    def push(self, src, dst, index, peer):
        copy = remote(src, dst, self.send.at[index], self.recv.at[index], peer)
        copy.start()
        self.sent.append(copy)

    def arrive(self, view, index):
        pltpu.make_async_copy(view, view, self.recv.at[index]).wait()

    def pairs(self):
        return [(dz, dy) for dy in range(self.g.Y) for dz in range(self.g.Z) if dz + dy > 0]

    def slot(self, dz, dy):
        return dz * self.g.Y + dy - 1

    def begin(self):
        g = self.g
        own = self.src.at[pl.ds(self.row, self.rows), self.mine]
        for dz in range(1, g.Z):
            self.push(own, self.view(g.f, self.mine), self.z_base + dz - 1, g.z_peer(dz))
        for dy in range(1, g.Y):
            self.push(own, self.view(g.f, self.mine), self.y_base + dy - 1, g.y_peer(dy))

    def over_y(self):
        g = self.g
        for dz in range(1, g.Z):
            shard = g.source(dz, 0)
            self.arrive(self.view(shard, self.mine), self.z_base + dz - 1)
            for dy in range(1, g.Y):
                self.push(
                    self.view(shard, self.mine),
                    self.view(shard, self.mine),
                    self.y_base + dz * (g.Y - 1) + dy - 1,
                    g.y_peer(dy),
                )
            self.over_x(dz, 0)

    def over_x(self, dz, dy):
        g = self.g
        view = self.view(g.source(dz, dy), self.x_out)
        self.push(view, view, self.x_base + self.slot(dz, dy), g.x_peer())

    def finish_y(self):
        g = self.g
        for dz in range(g.Z):
            for dy in range(1, g.Y):
                shard = g.source(dz, dy)
                self.arrive(self.view(shard, self.mine), self.y_base + dz * (g.Y - 1) + dy - 1)
                self.over_x(dz, dy)

    def over_core(self):
        g = self.g
        for dz, dy in self.pairs():
            shard = g.source(dz, dy)
            self.arrive(self.view(shard, self.x_in), self.x_base + self.slot(dz, dy))
            view = self.view(shard, self.core_out)
            self.push(view, view, self.c_base + self.slot(dz, dy), g.core_peer())

    def finish(self):
        g = self.g
        for dz, dy in self.pairs():
            shard = g.source(dz, dy)
            self.arrive(self.view(shard, self.core_in), self.c_base + self.slot(dz, dy))

    def drain(self):
        for copy in self.sent:
            copy.wait_send()


def refs_count(pieces):
    return 1 + max(piece[0] for piece in pieces)


class Scatter:
    def __init__(self, grid, src, out, rows, col, width, apart, bufs, send, recv, local):
        g = self.g = grid
        self.src, self.out, self.rows = src, out, rows
        self.send, self.recv, self.local = send, recv, local
        self.half, self.apart = width // 2, apart
        self.shared = self.half - 2 * apart
        self.core_keep = lanes(col + g.c * self.half, self.half)
        self.core_give = lanes(col + (1 - g.c) * self.half, self.half)
        self.x_keep = lanes(g.x * (apart + self.shared), apart)
        self.x_give = lanes((1 - g.x) * (apart + self.shared), apart)
        self.kept = lanes(g.x * apart, apart + self.shared)
        self.out_keep, self.out_give = self.core_keep, self.core_give
        self.near, self.core_in, self.x_in, self.y_in, self.z_sum, self.z_in, self.f_out, self.f_in, self.e_out, self.far = bufs
        self.sent = []

    @staticmethod
    def buffers(grid, rows, width, apart):
        half = width // 2
        part = half - apart
        bf = jnp.bfloat16
        return [
            pltpu.VMEM((grid.F, rows, half), bf),
            pltpu.VMEM((grid.F, rows, half), bf),
            pltpu.VMEM((grid.F, rows, apart), bf),
            pltpu.VMEM((grid.Y, grid.Z, rows, part), bf),
            pltpu.VMEM((grid.Z, rows, part), bf),
            pltpu.VMEM((grid.Z, rows, part), bf),
            pltpu.VMEM((rows, part), bf),
            pltpu.VMEM((rows, part), bf),
            pltpu.VMEM((2, rows, half), bf),
            pltpu.VMEM((grid.H, rows, part), bf),
        ]

    @staticmethod
    def count(grid):
        return 4 + grid.Z * (grid.Y - 1) + grid.Z - 1 + grid.H - 1

    def push(self, src, dst, index, peer):
        copy = remote(src, dst, self.send.at[index], self.recv.at[index], peer)
        copy.start()
        self.sent.append(copy)

    def arrive(self, view, index):
        pltpu.make_async_copy(view, view, self.recv.at[index]).wait()

    def begin(self):
        self.own = pltpu.make_async_copy(self.src.at[:, self.rows, self.core_keep], self.near, self.local)
        self.own.start()
        self.push(self.src.at[:, self.rows, self.core_give], self.core_in, 0, self.g.core_peer())

    def add(self, count, body):
        def step(i, carry):
            body(i)
            return carry

        lax.fori_loop(0, count, step, 0)

    def over_x(self):
        self.own.wait()
        self.arrive(self.core_in, 0)

        def body(i):
            self.near[i] = plus(self.near[i], self.core_in[i])

        self.add(self.g.F, body)
        self.push(self.near.at[:, :, self.x_give], self.x_in, 1, self.g.x_peer())

    def over_y(self):
        g = self.g
        self.arrive(self.x_in, 1)

        def body(i):
            self.near[i, :, self.x_keep] = plus(self.near[i, :, self.x_keep], self.x_in[i])

        self.add(g.F, body)
        for dz in range(g.Z):
            for dy in range(1, g.Y):
                self.push(
                    self.near.at[dz * g.Y + g.y_index(dy), :, self.kept],
                    self.y_in.at[dy, dz],
                    4 + dz * (g.Y - 1) + dy - 1,
                    g.y_peer(dy),
                )

    def over_z(self):
        g = self.g
        for dz in range(g.Z):
            for dy in range(1, g.Y):
                self.arrive(self.y_in.at[dy, dz], 4 + dz * (g.Y - 1) + dy - 1)

        def body(i):
            total = self.near[i * g.Y + g.y, :, self.kept].astype(jnp.float32)
            for dy in range(1, g.Y):
                total += self.y_in[dy, i].astype(jnp.float32)
            self.z_sum[i] = total.astype(jnp.bfloat16)

        self.add(g.Z, body)
        for dz in range(1, g.Z):
            self.push(
                self.z_sum.at[g.z_index(dz)],
                self.z_in.at[dz],
                4 + g.Z * (g.Y - 1) + dz - 1,
                g.z_peer(dz),
            )

    def over_pair(self):
        g = self.g
        for dz in range(1, g.Z):
            self.arrive(self.z_in.at[dz], 4 + g.Z * (g.Y - 1) + dz - 1)
        total = self.z_sum[g.z].astype(jnp.float32)
        for dz in range(1, g.Z):
            total += self.z_in[dz].astype(jnp.float32)
        self.f_out[...] = total.astype(jnp.bfloat16)
        if g.H > 1:
            self.over_far()
        self.push(self.f_out, self.f_in, 2, g.x_peer())

    def over_far(self):
        g = self.g
        base = 4 + g.Z * (g.Y - 1) + g.Z - 2
        self.far[g.h] = self.f_out[...]
        for dh in range(1, g.H):
            self.push(self.f_out, self.far.at[g.h], base + dh, g.far_peer(dh))
        for dh in range(1, g.H):
            self.arrive(self.far.at[g.far_index(-dh)], base + dh)
        for copy in self.sent[1 - g.H :]:
            copy.wait_send()
        del self.sent[1 - g.H :]
        total = self.far[0].astype(jnp.float32)
        for h in range(1, g.H):
            total += self.far[h].astype(jnp.float32)
        self.f_out[...] = total.astype(jnp.bfloat16)

    def over_core(self):
        g = self.g
        self.arrive(self.f_in, 2)
        shared_out = lanes((1 - g.x) * self.apart, self.shared)
        shared_in = lanes(g.x * self.apart, self.shared)
        own = lanes(g.x * self.shared, self.apart)
        other = lanes((1 - g.x) * self.shared, self.apart)
        e = self.e_out.at[0]
        e[:, lanes(self.apart, self.shared)] = plus(self.f_out[:, shared_out], self.f_in[:, shared_in])
        e[:, self.x_keep] = self.f_out[:, own]
        e[:, self.x_give] = self.f_in[:, other]
        self.push(e, self.e_out.at[1], 3, g.core_peer())

    def finish(self):
        self.arrive(self.e_out.at[1], 3)
        self.out[self.rows, self.out_keep] = self.e_out[0].astype(jnp.float32)
        self.out[self.rows, self.out_give] = self.e_out[1].astype(jnp.float32)

    def drain(self):
        for copy in self.sent:
            copy.wait_send()


def plus(left, right):
    return (left.astype(jnp.float32) + right.astype(jnp.float32)).astype(jnp.bfloat16)


def scatter_kernel(grid, pieces, *refs):
    n = len(pieces)
    count = refs_count(pieces)
    sources, outs = refs[:count], refs[count : 2 * count]
    bufs = refs[2 * count : 2 * count + 10 * n]
    send, recv, local = refs[2 * count + 10 * n :]
    grid.locate()
    grid.greet()
    chunks = [
        Scatter(
            grid,
            sources[which],
            outs[which],
            pl.ds(row, rows),
            col,
            width,
            apart,
            bufs[10 * i : 10 * i + 10],
            send.at[i],
            recv.at[i],
            local.at[i],
        )
        for i, (which, row, rows, col, width, apart) in enumerate(pieces)
    ]
    for chunk in chunks:
        chunk.begin()
    stages = ["over_x", "over_y", "over_z", "over_pair", "over_core", "finish"]
    for step in range(n + len(stages) - 1):
        for depth, stage in enumerate(stages):
            if 0 <= step - depth < n:
                getattr(chunks[step - depth], stage)()
    for chunk in chunks:
        chunk.drain()


def scatter_all(fsdp, dp, arrays):
    grid = Grid(fsdp, dp)
    pieces = []
    for which, array in enumerate(arrays):
        rows, width = array.shape[1:]
        if width == 3072:
            pieces += [(which, 0, rows, col, 1536, 128) for col in (0, 1536)]
        elif width == 2304:
            pieces += [(which, 0, rows, 0, 1536, 128), (which, 0, rows, 1536, 768, 128)]
        elif rows * fsdp > 768:
            pieces += [(which, row, rows // 2, 0, width, 128) for row in (0, rows // 2)]
        else:
            pieces.append((which, 0, rows, 0, width, 128))
    count = Scatter.count(grid)
    hbm = pl.BlockSpec(memory_space=pltpu.HBM)
    vmem = pl.BlockSpec(memory_space=pltpu.VMEM)
    scratch = []
    for _, _, rows, _, width, apart in pieces:
        scratch += Scatter.buffers(grid, rows, width, apart)
    return pl.pallas_call(
        functools.partial(scatter_kernel, grid, pieces),
        out_shape=[jax.ShapeDtypeStruct(a.shape[1:], jnp.float32) for a in arrays],
        in_specs=[hbm] * len(arrays),
        out_specs=[vmem] * len(arrays),
        scratch_shapes=scratch
        + [
            pltpu.SemaphoreType.DMA((len(pieces), count)),
            pltpu.SemaphoreType.DMA((len(pieces), count)),
            pltpu.SemaphoreType.DMA((len(pieces),)),
        ],
        compiler_params=pltpu.CompilerParams(
            collective_id=1, has_side_effects=True, vmem_limit_bytes=56 * 1024 * 1024
        ),
        name="scatter_gradients",
    )(*arrays)


NORM_EPSILON = 1e-06
PAD = 288
LOW = jnp.bfloat16
WIDE = jnp.float32
SMALL = ("gain_one", "shift_one", "heads", "project", "gain_two", "shift_two", "expand", "shrink")


def dot(left, right):
    return jnp.dot(left, right, preferred_element_type=WIDE)


def dot_t(left, right):
    return lax.dot_general(left, right, (((1,), (1,)), ((), ())), preferred_element_type=WIDE)


def t_dot(left, right):
    return lax.dot_general(left, right, (((0,), (0,)), ((), ())), preferred_element_type=WIDE)


def padded_rows(value, length):
    wide = value.astype(WIDE)
    if length == PAD:
        return wide
    return jnp.concatenate([wide, jnp.zeros((PAD - length, wide.shape[1]), WIDE)], axis=0)


def centre(wide):
    centred = wide - jnp.mean(wide, axis=-1, keepdims=True)
    scale = lax.rsqrt(jnp.mean(centred * centred, axis=-1, keepdims=True) + NORM_EPSILON)
    return centred * scale, scale


def norm_back(grad, normed, scale, gain):
    inner = grad * gain
    return scale * (
        inner
        - jnp.mean(inner, axis=-1, keepdims=True)
        - normed * jnp.mean(inner * normed, axis=-1, keepdims=True)
    )


def gelu_parts(value):
    bell = jnp.exp(value * value * -0.5)
    t = 1.0 / (1.0 + jnp.abs(value) * (0.3275911 * 0.7071067811865476))
    poly = t * (
        0.5 * 0.254829592
        + t
        * (
            0.5 * -0.284496736
            + t * (0.5 * 1.421413741 + t * (0.5 * -1.453152027 + t * (0.5 * 1.061405429)))
        )
    )
    tail = poly * bell
    return jnp.where(value >= 0, 1.0 - tail, tail), value * bell * 0.3989422804014327


def unpack_small(fsdp, packed, vectors):
    first = jnp.zeros((8, 768), WIDE)
    heads = [jnp.zeros((8, 768), WIDE) for _ in range(2)]
    hidden = [jnp.zeros((8, 768), WIDE) for _ in range(4)]
    for f in range(fsdp):
        rows = packed[pl.ds(8 * f, 8), :].astype(WIDE)

        def turned(length):
            start = f * length // fsdp
            return start // 768, (pltpu.roll(rows, start % 768, 1) if start % 768 else rows)

        _, value = turned(768)
        first += value
        part, value = turned(1536)
        heads[part] += value
        part, value = turned(3072)
        hidden[part] += value
    vectors[0:8, :] = first
    vectors[2:3, :] = heads[0][2:3]
    vectors[8:9, :] = heads[1][2:3]
    for part in range(4):
        vectors[9 + part : 10 + part, :] = hidden[part][6:7]


def attend(keep_bias, qkv, context, lse, base, width):
    first = lax.broadcasted_iota(jnp.int32, (1, 128), 1) < 64

    def heads(step, carry):
        at = pl.multiple_of(step * 128, 128)
        rows = pl.ds(base, PAD)
        query = qkv[rows, pl.ds(at, 128)] * LOW(0.125)
        key = qkv[rows, pl.ds(at + width, 128)]
        value = qkv[rows, pl.ds(at + 2 * width, 128)]
        outs = []
        for head in range(2):
            chosen = first if head == 0 else ~first
            scores = dot_t(jnp.where(chosen, query, LOW(0)), key) + keep_bias
            top = jnp.max(scores, axis=-1, keepdims=True)
            expo = jnp.exp(scores - top)
            total = jnp.sum(expo, axis=-1, keepdims=True)
            outs.append((dot(expo.astype(LOW), value) * (1.0 / total), top + jnp.log(total)))
        context[rows, pl.ds(at, 128)] = jnp.where(first, outs[0][0], outs[1][0]).astype(LOW)
        lse[rows, pl.ds(at, 128)] = jnp.where(first, outs[0][1], outs[1][1])
        return carry

    return heads


def forward_kernel(grid, sizes, counts, *refs):
    pairs, length, width, hidden = sizes
    (
        inputs,
        cotangent,
        packed_in,
        triple_in,
        project_in,
        expand_in,
        shrink_in,
        layer_out,
        normed_out,
        qkv_out,
        context_out,
        lse_out,
        middle_grad_out,
        context_grad_out,
        triple_out,
        vectors_out,
        sums_out,
        shrink_grad_out,
        expand_grad_out,
        project_grad_out,
        packed,
        triple,
        project,
        expand,
        shrink,
        vectors,
        sums,
        normed,
        qkv,
        context,
        lse,
        normed_two,
        upstream,
        branch,
        activated,
        pre_grad,
        stage_out,
        stage_ctx,
        send,
        recv,
        local,
        out_sem,
    ) = refs
    g = grid.locate()
    fsdp = grid.F
    sources = (packed_in, triple_in, project_in, expand_in, shrink_in)
    wholes = (packed, triple, project, expand, shrink)
    owns = []
    for index in range(5):
        depth = sources[index].shape[0]
        own = pltpu.make_async_copy(
            sources[index],
            wholes[index].at[pl.ds(pl.multiple_of(g.f * depth, 8), depth)],
            local.at[index],
        )
        own.start()
        owns.append(own)
    grid.greet()
    shrink_rows = shrink_in.shape[0]
    plan = [(0, 0, 8, 0, 768)]
    plan += [(1, 0, triple_in.shape[0], col, 768) for col in range(0, 3 * width, 768)]
    plan += [(2, 0, project_in.shape[0], 0, width)]
    plan += [(3, 0, expand_in.shape[0], col, hidden // 2) for col in (0, hidden // 2)]
    plan += [(4, row, shrink_rows // 2, 0, width) for row in (0, shrink_rows // 2)]
    chunks = [
        Gather(
            grid,
            sources[which],
            wholes[which],
            sources[which].shape[0],
            row,
            rows,
            col,
            span,
            send.at[i],
            recv.at[i],
        )
        for i, (which, row, rows, col, span) in enumerate(plan)
    ]
    n = len(chunks)
    ahead = 4

    def turn(step):
        if step + ahead < n:
            chunks[step + ahead].begin()
        if step < n:
            chunks[step].over_y()
        if 0 <= step - 1 < n:
            chunks[step - 1].finish_y()
        if 0 <= step - 2 < n:
            chunks[step - 2].over_core()

    for i in range(ahead):
        chunks[i].begin()
    writes = []

    def write(src, dst, index):
        copy = pltpu.make_async_copy(src, dst, out_sem.at[index])
        copy.start()
        writes.append(copy)

    for step in range(3):
        turn(step)
    owns[0].wait()
    chunks[0].finish()
    unpack_small(fsdp, packed, vectors)
    sums[...] = jnp.zeros_like(sums)
    write(vectors, vectors_out, 0)

    def vector(row, rows=1):
        return vectors[row : row + rows, :]

    def norm_one(b, carry):
        at = pl.multiple_of(b * PAD, 32)
        value, _ = centre(padded_rows(inputs[b], length))
        normed[pl.ds(at, PAD), :] = (value * vector(0) + vector(1)).astype(LOW)
        return carry

    turn(3)
    lax.fori_loop(0, pairs, norm_one, 0)
    write(normed, normed_out, 1)
    turn(4)
    turn(5)
    owns[1].wait()
    for i in range(1, 4):
        chunks[i].finish()
    write(triple, triple_out, 2)
    left = list(range(6, n + 2))
    per_pair = -(-len(left) // pairs)

    for b in range(pairs):
        base = b * PAD
        rows = pl.ds(base, PAD)
        for part in range(3):
            cols = pl.ds(part * width, width)
            bias = vector(2) if part == 0 else vector(8)
            value = dot(normed[rows, :], triple[:, cols])
            qkv[rows, cols] = (value if part == 1 else value + bias).astype(LOW)
        limit = TEXT + counts[b]
        keep = lax.broadcasted_iota(jnp.int32, (1, PAD), 1) < limit
        body = attend(jnp.where(keep, 0.0, -1e30), qkv, context, lse, base, width)
        lax.fori_loop(0, width // 128, body, 0)
        for _ in range(per_pair):
            if left:
                turn(left.pop(0))
    write(qkv, qkv_out, 3)
    write(context, context_out, 4)
    write(lse, lse_out, 5)
    for step in left:
        turn(step)
    for own in owns[2:]:
        own.wait()
    for i in range(4, n):
        chunks[i].finish()

    for chunk in chunks:
        chunk.drain()
    writes[-1].wait()
    stage_mid, stage_shrink, stage_expand = lse, shrink, expand
    block = hidden // 3

    def feed(b, carry):
        at = pl.multiple_of(b * PAD, 32)
        rows = pl.ds(at, PAD)
        limit = TEXT + counts[b]
        valid = lax.broadcasted_iota(jnp.int32, (PAD, 1), 0) < limit
        middle = padded_rows(inputs[b], length) + dot(context[rows, :], project[...]) + vector(3)
        value, scale = centre(middle)
        second = (value * vector(4) + vector(5)).astype(LOW)
        normed_two[rows, :] = second
        above = jnp.where(valid, padded_rows(cotangent[b], length), 0.0)
        above_low = above.astype(LOW)
        upstream[rows, :] = above_low
        mixed = jnp.zeros((PAD, width), WIDE)
        back = jnp.zeros((PAD, width), WIDE)
        for part in range(3):
            cols = slice(part * block, (part + 1) * block)
            bias = jnp.concatenate([vector(9 + i) for i in range(4)], axis=1)[:, cols]
            pre = dot(second, expand[:, cols]) + bias
            act_grad = dot_t(above_low, shrink[cols, :])
            share, slope = gelu_parts(pre)
            act = (pre * share).astype(LOW)
            activated[rows, cols] = act
            grad = (act_grad * (share + slope)).astype(LOW)
            pre_grad[rows, cols] = grad
            mixed += dot(act, shrink[cols, :])
            back += dot_t(grad, expand[:, cols])
            sums[0:1, cols] += jnp.sum(grad.astype(WIDE), axis=0, keepdims=True)
        layer = jnp.where(valid, middle + mixed + vector(7), 0.0)
        stage_out[b] = layer[:length].astype(LOW)
        middle_grad = above + norm_back(back, value, scale, vector(4))
        stage_mid[rows, :] = middle_grad
        low_grad = middle_grad.astype(LOW)
        branch[rows, :] = low_grad
        stage_ctx[rows, :] = dot_t(low_grad, project[...]).astype(LOW)
        for row, term in (
            (1, above),
            (2, low_grad.astype(WIDE)),
            (3, back * value),
            (4, back),
        ):
            sums[row : row + 1, 0:width] += jnp.sum(term, axis=0, keepdims=True)
        return carry

    lax.fori_loop(0, pairs, feed, 0)
    write(stage_out, layer_out, 6)
    write(stage_mid, middle_grad_out, 7)
    write(stage_ctx, context_grad_out, 8)
    write(sums, sums_out, 9)

    def shrink_grad(i, carry):
        at = pl.multiple_of(i * 384, 384)
        stage_shrink[pl.ds(at, 384), :] = t_dot(
            activated[:, pl.ds(at, 384)], upstream[...]
        ).astype(LOW)
        return carry

    lax.fori_loop(0, hidden // 384, shrink_grad, 0)
    write(stage_shrink, shrink_grad_out, 10)

    def expand_grad(i, carry):
        at = pl.multiple_of(i * 256, 256)
        for part in range(3):
            cols = slice(part * block, (part + 1) * block)
            stage_expand[pl.ds(at, 256), cols] = t_dot(
                normed_two[:, pl.ds(at, 256)], pre_grad[:, cols]
            ).astype(LOW)
        return carry

    lax.fori_loop(0, width // 256, expand_grad, 0)
    write(stage_expand, expand_grad_out, 11)
    for copy in writes[2:3]:
        copy.wait()
    project_stage = triple.at[:, pl.ds(0, width)]

    def project_grad(i, carry):
        at = pl.multiple_of(i * 256, 256)
        project_stage[pl.ds(at, 256), :] = t_dot(context[:, pl.ds(at, 256)], branch[...]).astype(LOW)
        return carry

    lax.fori_loop(0, width // 256, project_grad, 0)
    write(project_stage, project_grad_out, 12)
    for i, copy in enumerate(writes):
        if i not in (2, 5):
            copy.wait()


def run_forward(fsdp, dp, counts, inputs, cotangent, packed, triple, project, expand, shrink):
    grid = Grid(fsdp, dp)
    pairs, length, width = inputs.shape
    hidden = expand.shape[1]
    rows = pairs * PAD
    hbm = pl.BlockSpec(memory_space=pltpu.HBM)
    vmem = pl.BlockSpec(memory_space=pltpu.VMEM)
    count = Gather.count(grid)
    shape = jax.ShapeDtypeStruct
    outs = [
        shape((pairs, length, width), LOW),
        shape((rows, width), LOW),
        shape((rows, 3 * width), LOW),
        shape((rows, width), LOW),
        shape((rows, width), WIDE),
        shape((rows, width), WIDE),
        shape((rows, width), LOW),
        shape((width, 3 * width), LOW),
        shape((16, width), WIDE),
        shape((8, hidden), WIDE),
        shape((hidden, width), LOW),
        shape((width, hidden), LOW),
        shape((width, width), LOW),
    ]
    scratch = [
        pltpu.VMEM((fsdp * 8, 768), LOW),
        pltpu.VMEM((width, 3 * width), LOW),
        pltpu.VMEM((width, width), LOW),
        pltpu.VMEM((width, hidden), LOW),
        pltpu.VMEM((hidden, width), LOW),
        pltpu.VMEM((16, width), WIDE),
        pltpu.VMEM((8, hidden), WIDE),
        pltpu.VMEM((rows, width), LOW),
        pltpu.VMEM((rows, 3 * width), LOW),
        pltpu.VMEM((rows, width), LOW),
        pltpu.VMEM((rows, width), WIDE),
        pltpu.VMEM((rows, width), LOW),
        pltpu.VMEM((rows, width), LOW),
        pltpu.VMEM((rows, width), LOW),
        pltpu.VMEM((rows, hidden), LOW),
        pltpu.VMEM((rows, hidden), LOW),
        pltpu.VMEM((pairs, length, width), LOW),
        pltpu.VMEM((rows, width), LOW),
        pltpu.SemaphoreType.DMA((9, count)),
        pltpu.SemaphoreType.DMA((9, count)),
        pltpu.SemaphoreType.DMA((5,)),
        pltpu.SemaphoreType.DMA((13,)),
    ]
    return pl.pallas_call(
        functools.partial(forward_kernel, grid, (pairs, length, width, hidden)),
        out_shape=outs,
        in_specs=[pl.BlockSpec(memory_space=pltpu.SMEM), vmem, vmem] + [hbm] * 5,
        out_specs=[hbm] * len(outs),
        scratch_shapes=scratch,
        compiler_params=pltpu.CompilerParams(
            collective_id=0, has_side_effects=True, vmem_limit_bytes=63 * 1024 * 1024
        ),
        name="forward_and_feed_back",
    )(counts, inputs, cotangent, packed, triple, project, expand, shrink)


def shards(
    inputs,
    patch_count,
    cotangent,
    first_gain,
    first_shift,
    triple_weight,
    head_bias,
    output_weight,
    output_bias,
    second_gain,
    second_shift,
    expand_weight,
    expand_bias,
    reduce_weight,
    reduce_bias,
):
    fsdp, dp = lax.axis_size("fsdp"), lax.axis_size("dp")
    small = (
        first_gain,
        first_shift,
        head_bias,
        output_bias,
        second_gain,
        second_shift,
        expand_bias,
        reduce_bias,
    )
    packed = jnp.stack([jnp.pad(item, (0, 768 - item.shape[0])) for item in small])
    (
        layer_output,
        hidden_one,
        triple_rows,
        context,
        lse,
        middle_grad,
        context_grad,
        triple,
        vectors,
        sums,
        shrink_grad,
        expand_grad,
        project_grad,
    ) = run_forward(
        fsdp,
        dp,
        patch_count,
        inputs,
        cotangent,
        packed,
        triple_weight,
        output_weight,
        expand_weight,
        reduce_weight,
    )
    pairs, length, width = inputs.shape
    gain_one = vectors[0]

    def rows(value):
        return value.reshape(pairs, PAD, -1)[:, :length]

    triple_rows, lse, middle_grad, context_grad, hidden_one = (
        rows(item) for item in (triple_rows, lse, middle_grad, context_grad, hidden_one)
    )
    inputs_wide = inputs.astype(WIDE)
    query_rows, key_rows, value_rows = (
        triple_rows[..., i * width : (i + 1) * width].reshape(pairs, length, HEADS, HEAD_DIM)
        for i in range(3)
    )
    context_grad = context_grad.reshape(pairs, length, HEADS, HEAD_DIM)
    row_lse = lse.reshape(pairs, length, HEADS, HEAD_DIM)[..., 0].transpose(0, 2, 1)[..., None]
    positions = lax.broadcasted_iota(jnp.int32, (pairs, length), 1)
    key_mask = (positions < TEXT + patch_count[:, None])[:, None, None, :]
    scores = jnp.einsum("pshd,pthd->phst", query_rows, key_rows, preferred_element_type=WIDE) * 0.125
    probs_again = jnp.exp(jnp.where(key_mask, scores, -1e30) - row_lse)
    value_grad = jnp.einsum(
        "phst,pshd->pthd", probs_again.astype(LOW), context_grad, preferred_element_type=WIDE
    )
    probs_grad = jnp.einsum(
        "pshd,pthd->phst", context_grad, value_rows, preferred_element_type=WIDE
    )
    score_grad = (
        probs_again * (probs_grad - jnp.sum(probs_again * probs_grad, axis=-1, keepdims=True))
    ).astype(LOW)
    query_grad = (
        jnp.einsum("phst,pthd->pshd", score_grad, key_rows, preferred_element_type=WIDE) * 0.125
    )
    key_grad = (
        jnp.einsum("phst,pshd->pthd", score_grad, query_rows, preferred_element_type=WIDE) * 0.125
    )
    triple_grad_rows = jnp.concatenate(
        [item.reshape(pairs, length, width) for item in (query_grad, key_grad, value_grad)], axis=-1
    ).astype(LOW)
    bias_sums = jnp.sum(triple_grad_rows.astype(WIDE), axis=(0, 1))
    head_bias_grad = jnp.concatenate([bias_sums[:width], bias_sums[2 * width :]])
    triple_grad = jnp.einsum("psd,pse->de", hidden_one, triple_grad_rows, preferred_element_type=WIDE)
    hidden_one_grad = jnp.einsum(
        "pse,de->psd", triple_grad_rows, triple, preferred_element_type=WIDE
    )
    normed, scale = centre(inputs_wide)
    gain_one_grad = jnp.sum(hidden_one_grad * normed, axis=(0, 1))
    shift_one_grad = jnp.sum(hidden_one_grad, axis=(0, 1))
    input_gradient = (middle_grad + norm_back(hidden_one_grad, normed, scale, gain_one)).astype(LOW)
    small_grads = (
        gain_one_grad,
        shift_one_grad,
        head_bias_grad,
        sums[2, :width],
        sums[3, :width],
        sums[4, :width],
        sums[0],
        sums[1, :width],
    )
    packed_grad = jnp.stack(
        [
            jnp.pad(
                item.astype(LOW).reshape(fsdp, -1), ((0, 0), (0, 768 - item.shape[0] // fsdp))
            )
            for item in small_grads
        ],
        axis=1,
    )
    shares = scatter_all(
        fsdp,
        dp,
        tuple(
            item.astype(LOW).reshape(fsdp, -1, item.shape[-1])
            for item in (shrink_grad, expand_grad, project_grad, triple_grad)
        )
        + (packed_grad,),
    )
    (
        gain_one_sum,
        shift_one_sum,
        head_bias_sum,
        project_bias_sum,
        gain_two_sum,
        shift_two_sum,
        expand_add_sum,
        shrink_add_sum,
    ) = (shares[4][index, : item.shape[0] // fsdp] for index, item in enumerate(small_grads))
    return (
        layer_output,
        input_gradient,
        gain_one_sum,
        shift_one_sum,
        shares[3],
        head_bias_sum,
        shares[2],
        project_bias_sum,
        gain_two_sum,
        shift_two_sum,
        shares[1],
        expand_add_sum,
        shares[0],
        shrink_add_sum,
    )


def solution(mesh):
    in_specs = (
        P(("dp", "fsdp"), None, None),
        P(("dp", "fsdp")),
        P(("dp", "fsdp"), None, None),
        P("fsdp"),
        P("fsdp"),
        P("fsdp", None),
        P("fsdp"),
        P("fsdp", None),
        P("fsdp"),
        P("fsdp"),
        P("fsdp"),
        P("fsdp", None),
        P("fsdp"),
        P("fsdp", None),
        P("fsdp"),
    )
    out_specs = (
        P(("dp", "fsdp"), None, None),
        P(("dp", "fsdp"), None, None),
        P("fsdp"),
        P("fsdp"),
        P("fsdp", None),
        P("fsdp"),
        P("fsdp", None),
        P("fsdp"),
        P("fsdp"),
        P("fsdp"),
        P("fsdp", None),
        P("fsdp"),
        P("fsdp", None),
        P("fsdp"),
    )
    return jax.shard_map(shards, mesh=mesh, in_specs=in_specs, out_specs=out_specs, check_vma=False)
```

```python
import functools

import jax
import jax.numpy as jnp
from jax import lax
from jax.experimental import pallas as pl
from jax.experimental.pallas import tpu as pltpu
from jax.sharding import PartitionSpec as P

TEXT = 40
MESH = pl.DeviceIdType.MESH


class Grid:
    def __init__(self, fsdp, dp):
        self.H = dp // 4
        y_size = 1
        while y_size * y_size * 8 <= fsdp:
            y_size *= 2
        self.F, self.Y, self.Z = fsdp, y_size, fsdp // y_size

    def locate(self):
        self.dp = lax.axis_index("dp")
        self.f = lax.axis_index("fsdp")
        self.c = lax.rem(self.dp, 2)
        self.x = lax.rem(self.dp // 2, 2)
        self.h = self.dp // 4
        self.z = self.f // self.Y
        self.y = lax.rem(self.f, self.Y)
        return self

    def core_peer(self):
        return (self.dp + 1 - 2 * self.c, self.f)

    def x_peer(self):
        return (self.dp + 2 - 4 * self.x, self.f)

    def far_index(self, dh):
        return lax.rem(self.h + self.H + dh, self.H)

    def far_peer(self, dh):
        return (self.far_index(dh) * 4 + lax.rem(self.dp, 4), self.f)

    def z_index(self, dz):
        return lax.rem(self.z + self.Z + dz, self.Z)

    def y_index(self, dy):
        return lax.rem(self.y + self.Y + dy, self.Y)

    def z_peer(self, dz):
        return (self.dp, self.z_index(dz) * self.Y + self.y)

    def y_peer(self, dy):
        return (self.dp, self.z * self.Y + self.y_index(dy))

    def source(self, dz, dy):
        return self.z_index(-dz) * self.Y + self.y_index(-dy)

    def greet(self):
        barrier = pltpu.get_barrier_semaphore()
        peers = [self.core_peer(), self.x_peer()]
        peers += [self.z_peer(dz) for dz in range(1, self.Z)]
        peers += [self.y_peer(dy) for dy in range(1, self.Y)]
        peers += [self.far_peer(dh) for dh in range(1, self.H)]
        for peer in peers:
            pl.semaphore_signal(barrier, inc=1, device_id=peer, device_id_type=MESH)
        pl.semaphore_wait(barrier, len(peers))


def remote(src, dst, send, recv, peer):
    return pltpu.make_async_remote_copy(
        src_ref=src,
        dst_ref=dst,
        send_sem=send,
        recv_sem=recv,
        device_id=peer,
        device_id_type=MESH,
    )


def lanes(start, width):
    return pl.ds(pl.multiple_of(start, 128), width)


class Gather:
    def __init__(self, grid, src, dst, depth, row, rows, col, width, send, recv):
        self.g, self.src, self.dst = grid, src, dst
        self.depth, self.row, self.rows = depth, row, rows
        self.send, self.recv = send, recv
        half, group = width // 2, width // 6
        self.sent = []
        g = grid
        self.mine = lanes(col + g.c * half + g.x * group, 2 * group)
        self.x_out = lanes(col + g.c * half + 2 * g.x * group, group)
        self.x_in = lanes(col + g.c * half + 2 * (1 - g.x) * group, group)
        self.core_out = lanes(col + g.c * half, half)
        self.core_in = lanes(col + (1 - g.c) * half, half)
        self.z_base, self.y_base = 0, g.Z - 1
        self.x_base = self.y_base + g.Z * (g.Y - 1)
        self.c_base = self.x_base + g.F - 1

    @staticmethod
    def count(grid):
        return grid.Z - 1 + grid.Z * (grid.Y - 1) + 2 * (grid.F - 1)

    def view(self, shard, columns):
        start = pl.multiple_of(shard * self.depth + self.row, 8)
        return self.dst.at[pl.ds(start, self.rows), columns]

    def push(self, src, dst, index, peer):
        copy = remote(src, dst, self.send.at[index], self.recv.at[index], peer)
        copy.start()
        self.sent.append(copy)

    def arrive(self, view, index):
        pltpu.make_async_copy(view, view, self.recv.at[index]).wait()

    def pairs(self):
        return [(dz, dy) for dy in range(self.g.Y) for dz in range(self.g.Z) if dz + dy > 0]

    def slot(self, dz, dy):
        return dz * self.g.Y + dy - 1

    def begin(self):
        g = self.g
        own = self.src.at[pl.ds(self.row, self.rows), self.mine]
        for dz in range(1, g.Z):
            self.push(own, self.view(g.f, self.mine), self.z_base + dz - 1, g.z_peer(dz))
        for dy in range(1, g.Y):
            self.push(own, self.view(g.f, self.mine), self.y_base + dy - 1, g.y_peer(dy))

    def over_y(self):
        g = self.g
        for dz in range(1, g.Z):
            shard = g.source(dz, 0)
            self.arrive(self.view(shard, self.mine), self.z_base + dz - 1)
            for dy in range(1, g.Y):
                self.push(
                    self.view(shard, self.mine),
                    self.view(shard, self.mine),
                    self.y_base + dz * (g.Y - 1) + dy - 1,
                    g.y_peer(dy),
                )
            self.over_x(dz, 0)

    def over_x(self, dz, dy):
        g = self.g
        view = self.view(g.source(dz, dy), self.x_out)
        self.push(view, view, self.x_base + self.slot(dz, dy), g.x_peer())

    def finish_y(self):
        g = self.g
        for dz in range(g.Z):
            for dy in range(1, g.Y):
                shard = g.source(dz, dy)
                self.arrive(self.view(shard, self.mine), self.y_base + dz * (g.Y - 1) + dy - 1)
                self.over_x(dz, dy)

    def over_core(self):
        g = self.g
        for dz, dy in self.pairs():
            shard = g.source(dz, dy)
            self.arrive(self.view(shard, self.x_in), self.x_base + self.slot(dz, dy))
            view = self.view(shard, self.core_out)
            self.push(view, view, self.c_base + self.slot(dz, dy), g.core_peer())

    def finish(self):
        g = self.g
        for dz, dy in self.pairs():
            shard = g.source(dz, dy)
            self.arrive(self.view(shard, self.core_in), self.c_base + self.slot(dz, dy))

    def drain(self):
        for copy in self.sent:
            copy.wait_send()


class Scatter:
    def __init__(self, grid, src, out, rows, col, width, apart, bufs, send, recv, local):
        g = self.g = grid
        self.src, self.out, self.rows = src, out, rows
        self.send, self.recv, self.local = send, recv, local
        self.half, self.apart = width // 2, apart
        self.shared = self.half - 2 * apart
        self.core_keep = lanes(col + g.c * self.half, self.half)
        self.core_give = lanes(col + (1 - g.c) * self.half, self.half)
        self.x_keep = lanes(g.x * (apart + self.shared), apart)
        self.x_give = lanes((1 - g.x) * (apart + self.shared), apart)
        self.kept = lanes(g.x * apart, apart + self.shared)
        self.out_keep, self.out_give = self.core_keep, self.core_give
        self.near, self.core_in, self.x_in, self.y_in, self.z_sum, self.z_in, self.f_out, self.f_in, self.e_out, self.far = bufs
        self.sent = []

    @staticmethod
    def buffers(grid, rows, width, apart):
        half = width // 2
        part = half - apart
        bf = jnp.bfloat16
        return [
            pltpu.VMEM((grid.F, rows, half), bf),
            pltpu.VMEM((grid.F, rows, half), bf),
            pltpu.VMEM((grid.F, rows, apart), bf),
            pltpu.VMEM((grid.Y, grid.Z, rows, part), bf),
            pltpu.VMEM((grid.Z, rows, part), bf),
            pltpu.VMEM((grid.Z, rows, part), bf),
            pltpu.VMEM((rows, part), bf),
            pltpu.VMEM((rows, part), bf),
            pltpu.VMEM((2, rows, half), bf),
            pltpu.VMEM((grid.H, rows, part), bf),
        ]

    @staticmethod
    def count(grid):
        return 4 + grid.Z * (grid.Y - 1) + grid.Z - 1 + grid.H - 1

    def push(self, src, dst, index, peer):
        copy = remote(src, dst, self.send.at[index], self.recv.at[index], peer)
        copy.start()
        self.sent.append(copy)

    def arrive(self, view, index):
        pltpu.make_async_copy(view, view, self.recv.at[index]).wait()

    def begin(self):
        self.own = pltpu.make_async_copy(self.src.at[:, self.rows, self.core_keep], self.near, self.local)
        self.own.start()
        self.push(self.src.at[:, self.rows, self.core_give], self.core_in, 0, self.g.core_peer())

    def add(self, count, body):
        def step(i, carry):
            body(i)
            return carry

        lax.fori_loop(0, count, step, 0)

    def over_x(self):
        self.own.wait()
        self.arrive(self.core_in, 0)

        def body(i):
            self.near[i] = plus(self.near[i], self.core_in[i])

        self.add(self.g.F, body)
        self.push(self.near.at[:, :, self.x_give], self.x_in, 1, self.g.x_peer())

    def over_y(self):
        g = self.g
        self.arrive(self.x_in, 1)

        def body(i):
            self.near[i, :, self.x_keep] = plus(self.near[i, :, self.x_keep], self.x_in[i])

        self.add(g.F, body)
        for dz in range(g.Z):
            for dy in range(1, g.Y):
                self.push(
                    self.near.at[dz * g.Y + g.y_index(dy), :, self.kept],
                    self.y_in.at[dy, dz],
                    4 + dz * (g.Y - 1) + dy - 1,
                    g.y_peer(dy),
                )

    def over_z(self):
        g = self.g
        for dz in range(g.Z):
            for dy in range(1, g.Y):
                self.arrive(self.y_in.at[dy, dz], 4 + dz * (g.Y - 1) + dy - 1)

        def body(i):
            total = self.near[i * g.Y + g.y, :, self.kept].astype(jnp.float32)
            for dy in range(1, g.Y):
                total += self.y_in[dy, i].astype(jnp.float32)
            self.z_sum[i] = total.astype(jnp.bfloat16)

        self.add(g.Z, body)
        for dz in range(1, g.Z):
            self.push(
                self.z_sum.at[g.z_index(dz)],
                self.z_in.at[dz],
                4 + g.Z * (g.Y - 1) + dz - 1,
                g.z_peer(dz),
            )

    def over_pair(self):
        g = self.g
        for dz in range(1, g.Z):
            self.arrive(self.z_in.at[dz], 4 + g.Z * (g.Y - 1) + dz - 1)
        total = self.z_sum[g.z].astype(jnp.float32)
        for dz in range(1, g.Z):
            total += self.z_in[dz].astype(jnp.float32)
        self.f_out[...] = total.astype(jnp.bfloat16)
        if g.H > 1:
            self.over_far()
        self.push(self.f_out, self.f_in, 2, g.x_peer())

    def over_far(self):
        g = self.g
        base = 4 + g.Z * (g.Y - 1) + g.Z - 2
        self.far[g.h] = self.f_out[...]
        for dh in range(1, g.H):
            self.push(self.f_out, self.far.at[g.h], base + dh, g.far_peer(dh))
        for dh in range(1, g.H):
            self.arrive(self.far.at[g.far_index(-dh)], base + dh)
        for copy in self.sent[1 - g.H :]:
            copy.wait_send()
        del self.sent[1 - g.H :]
        total = self.far[0].astype(jnp.float32)
        for h in range(1, g.H):
            total += self.far[h].astype(jnp.float32)
        self.f_out[...] = total.astype(jnp.bfloat16)

    def over_core(self):
        g = self.g
        self.arrive(self.f_in, 2)
        shared_out = lanes((1 - g.x) * self.apart, self.shared)
        shared_in = lanes(g.x * self.apart, self.shared)
        own = lanes(g.x * self.shared, self.apart)
        other = lanes((1 - g.x) * self.shared, self.apart)
        e = self.e_out.at[0]
        e[:, lanes(self.apart, self.shared)] = plus(self.f_out[:, shared_out], self.f_in[:, shared_in])
        e[:, self.x_keep] = self.f_out[:, own]
        e[:, self.x_give] = self.f_in[:, other]
        self.push(e, self.e_out.at[1], 3, g.core_peer())

    def finish(self):
        self.arrive(self.e_out.at[1], 3)
        self.out[self.rows, self.out_keep] = self.e_out[0]
        self.out[self.rows, self.out_give] = self.e_out[1]

    def drain(self):
        for copy in self.sent:
            copy.wait_send()


def plus(left, right):
    return (left.astype(jnp.float32) + right.astype(jnp.float32)).astype(jnp.bfloat16)


NORM_EPSILON = 1e-06
PAD = 288
LOW = jnp.bfloat16
WIDE = jnp.float32
SMALL = ("gain_one", "shift_one", "heads", "project", "gain_two", "shift_two", "expand", "shrink")


def dot(left, right):
    return jnp.dot(left, right, preferred_element_type=WIDE)


def dot_t(left, right):
    return lax.dot_general(left, right, (((1,), (1,)), ((), ())), preferred_element_type=WIDE)


def t_dot(left, right):
    return lax.dot_general(left, right, (((0,), (0,)), ((), ())), preferred_element_type=WIDE)


def padded_rows(value, length):
    wide = value.astype(WIDE)
    if length == PAD:
        return wide
    return jnp.concatenate([wide, jnp.zeros((PAD - length, wide.shape[1]), WIDE)], axis=0)


def centre(wide):
    centred = wide - jnp.mean(wide, axis=-1, keepdims=True)
    scale = lax.rsqrt(jnp.mean(centred * centred, axis=-1, keepdims=True) + NORM_EPSILON)
    return centred * scale, scale


def norm_back(grad, normed, scale, gain):
    inner = grad * gain
    return scale * (
        inner
        - jnp.mean(inner, axis=-1, keepdims=True)
        - normed * jnp.mean(inner * normed, axis=-1, keepdims=True)
    )


def gelu_parts(value):
    bell = jnp.exp(value * value * -0.5)
    t = 1.0 / (1.0 + jnp.abs(value) * (0.3275911 * 0.7071067811865476))
    poly = t * (
        0.5 * 0.254829592
        + t
        * (
            0.5 * -0.284496736
            + t * (0.5 * 1.421413741 + t * (0.5 * -1.453152027 + t * (0.5 * 1.061405429)))
        )
    )
    tail = poly * bell
    return jnp.where(value >= 0, 1.0 - tail, tail), value * bell * 0.3989422804014327


def unpack_small(fsdp, packed, vectors):
    first = jnp.zeros((8, 768), WIDE)
    heads = [jnp.zeros((8, 768), WIDE) for _ in range(2)]
    hidden = [jnp.zeros((8, 768), WIDE) for _ in range(4)]
    for f in range(fsdp):
        rows = packed[pl.ds(8 * f, 8), :].astype(WIDE)

        def turned(length):
            start = f * length // fsdp
            return start // 768, (pltpu.roll(rows, start % 768, 1) if start % 768 else rows)

        _, value = turned(768)
        first += value
        part, value = turned(1536)
        heads[part] += value
        part, value = turned(3072)
        hidden[part] += value
    vectors[0:8, :] = first
    vectors[2:3, :] = heads[0][2:3]
    vectors[8:9, :] = heads[1][2:3]
    for part in range(4):
        vectors[9 + part : 10 + part, :] = hidden[part][6:7]


def attend(keep_bias, qkv, context, lse, base, width):
    first = lax.broadcasted_iota(jnp.int32, (1, 128), 1) < 64

    def heads(step, carry):
        at = pl.multiple_of(step * 128, 128)
        rows = pl.ds(base, PAD)
        query = qkv[rows, pl.ds(at, 128)] * LOW(0.125)
        key = qkv[rows, pl.ds(at + width, 128)]
        value = qkv[rows, pl.ds(at + 2 * width, 128)]
        outs = []
        for head in range(2):
            chosen = first if head == 0 else ~first
            scores = dot_t(jnp.where(chosen, query, LOW(0)), key) + keep_bias
            top = jnp.max(scores, axis=-1, keepdims=True)
            expo = jnp.exp(scores - top)
            total = jnp.sum(expo, axis=-1, keepdims=True)
            outs.append((dot(expo.astype(LOW), value) * (1.0 / total), top + jnp.log(total)))
        context[rows, pl.ds(at, 128)] = jnp.where(first, outs[0][0], outs[1][0]).astype(LOW)
        lse[rows, pl.ds(at, 128)] = jnp.where(first, outs[0][1], outs[1][1])
        return carry

    return heads


def forward_kernel(grid, sizes, counts, *refs):
    pairs, length, width, hidden = sizes
    (
        inputs,
        cotangent,
        packed_in,
        triple_in,
        project_in,
        expand_in,
        shrink_in,
        layer_out,
        normed_out,
        qkv_out,
        context_out,
        lse_out,
        middle_grad_out,
        context_grad_out,
        triple_out,
        vectors_out,
        sums_out,
        shrink_grad_out,
        expand_grad_out,
        project_grad_out,
        packed,
        triple,
        project,
        expand,
        shrink,
        vectors,
        sums,
        normed,
        qkv,
        context,
        lse,
        normed_two,
        upstream,
        branch,
        activated,
        pre_grad,
        stage_out,
        stage_ctx,
        send,
        recv,
        local,
        out_sem,
    ) = refs
    g = grid.locate()
    fsdp = grid.F
    sources = (packed_in, triple_in, project_in, expand_in, shrink_in)
    wholes = (packed, triple, project, expand, shrink)
    owns = []
    for index in range(5):
        depth = sources[index].shape[0]
        own = pltpu.make_async_copy(
            sources[index],
            wholes[index].at[pl.ds(pl.multiple_of(g.f * depth, 8), depth)],
            local.at[index],
        )
        own.start()
        owns.append(own)
    grid.greet()
    shrink_rows = shrink_in.shape[0]
    plan = [(0, 0, 8, 0, 768)]
    plan += [(1, 0, triple_in.shape[0], col, 768) for col in range(0, 3 * width, 768)]
    plan += [(2, 0, project_in.shape[0], 0, width)]
    plan += [(3, 0, expand_in.shape[0], col, hidden // 2) for col in (0, hidden // 2)]
    plan += [(4, row, shrink_rows // 2, 0, width) for row in (0, shrink_rows // 2)]
    chunks = [
        Gather(
            grid,
            sources[which],
            wholes[which],
            sources[which].shape[0],
            row,
            rows,
            col,
            span,
            send.at[i],
            recv.at[i],
        )
        for i, (which, row, rows, col, span) in enumerate(plan)
    ]
    n = len(chunks)
    ahead = 4

    def turn(step):
        if step + ahead < n:
            chunks[step + ahead].begin()
        if step < n:
            chunks[step].over_y()
        if 0 <= step - 1 < n:
            chunks[step - 1].finish_y()
        if 0 <= step - 2 < n:
            chunks[step - 2].over_core()

    for i in range(ahead):
        chunks[i].begin()
    writes = []

    def write(src, dst, index):
        copy = pltpu.make_async_copy(src, dst, out_sem.at[index])
        copy.start()
        writes.append(copy)

    for step in range(3):
        turn(step)
    owns[0].wait()
    chunks[0].finish()
    unpack_small(fsdp, packed, vectors)
    sums[...] = jnp.zeros_like(sums)
    write(vectors, vectors_out, 0)

    def vector(row, rows=1):
        return vectors[row : row + rows, :]

    def norm_one(b, carry):
        at = pl.multiple_of(b * PAD, 32)
        value, _ = centre(padded_rows(inputs[b], length))
        normed[pl.ds(at, PAD), :] = (value * vector(0) + vector(1)).astype(LOW)
        return carry

    turn(3)
    lax.fori_loop(0, pairs, norm_one, 0)
    write(normed, normed_out, 1)
    turn(4)
    turn(5)
    owns[1].wait()
    for i in range(1, 4):
        chunks[i].finish()
    write(triple, triple_out, 2)
    left = list(range(6, n + 2))
    per_pair = -(-len(left) // pairs)

    for b in range(pairs):
        base = b * PAD
        rows = pl.ds(base, PAD)
        for part in range(3):
            cols = pl.ds(part * width, width)
            bias = vector(2) if part == 0 else vector(8)
            value = dot(normed[rows, :], triple[:, cols])
            qkv[rows, cols] = (value if part == 1 else value + bias).astype(LOW)
        limit = TEXT + counts[b]
        keep = lax.broadcasted_iota(jnp.int32, (1, PAD), 1) < limit
        body = attend(jnp.where(keep, 0.0, -1e30), qkv, context, lse, base, width)
        lax.fori_loop(0, width // 128, body, 0)
        for _ in range(per_pair):
            if left:
                turn(left.pop(0))
    write(qkv, qkv_out, 3)
    write(context, context_out, 4)
    write(lse, lse_out, 5)
    for step in left:
        turn(step)
    for own in owns[2:]:
        own.wait()
    for i in range(4, n):
        chunks[i].finish()

    for chunk in chunks:
        chunk.drain()
    writes[-1].wait()
    stage_mid, stage_shrink, stage_expand = lse, shrink, expand
    block = hidden // 3

    def feed(b, carry):
        at = pl.multiple_of(b * PAD, 32)
        rows = pl.ds(at, PAD)
        limit = TEXT + counts[b]
        valid = lax.broadcasted_iota(jnp.int32, (PAD, 1), 0) < limit
        middle = padded_rows(inputs[b], length) + dot(context[rows, :], project[...]) + vector(3)
        value, scale = centre(middle)
        second = (value * vector(4) + vector(5)).astype(LOW)
        normed_two[rows, :] = second
        above = jnp.where(valid, padded_rows(cotangent[b], length), 0.0)
        above_low = above.astype(LOW)
        upstream[rows, :] = above_low
        mixed = jnp.zeros((PAD, width), WIDE)
        back = jnp.zeros((PAD, width), WIDE)
        for part in range(3):
            cols = slice(part * block, (part + 1) * block)
            bias = jnp.concatenate([vector(9 + i) for i in range(4)], axis=1)[:, cols]
            pre = dot(second, expand[:, cols]) + bias
            act_grad = dot_t(above_low, shrink[cols, :])
            share, slope = gelu_parts(pre)
            act = (pre * share).astype(LOW)
            activated[rows, cols] = act
            grad = (act_grad * (share + slope)).astype(LOW)
            pre_grad[rows, cols] = grad
            mixed += dot(act, shrink[cols, :])
            back += dot_t(grad, expand[:, cols])
            sums[0:1, cols] += jnp.sum(grad.astype(WIDE), axis=0, keepdims=True)
        layer = jnp.where(valid, middle + mixed + vector(7), 0.0)
        stage_out[b] = layer[:length].astype(LOW)
        middle_grad = above + norm_back(back, value, scale, vector(4))
        stage_mid[rows, :] = middle_grad
        low_grad = middle_grad.astype(LOW)
        branch[rows, :] = low_grad
        stage_ctx[rows, :] = dot_t(low_grad, project[...]).astype(LOW)
        for row, term in (
            (1, above),
            (2, low_grad.astype(WIDE)),
            (3, back * value),
            (4, back),
        ):
            sums[row : row + 1, 0:width] += jnp.sum(term, axis=0, keepdims=True)
        return carry

    lax.fori_loop(0, pairs, feed, 0)
    write(stage_out, layer_out, 6)
    write(stage_mid, middle_grad_out, 7)
    write(stage_ctx, context_grad_out, 8)
    write(sums, sums_out, 9)

    def shrink_grad(i, carry):
        at = pl.multiple_of(i * 384, 384)
        stage_shrink[pl.ds(at, 384), :] = t_dot(
            activated[:, pl.ds(at, 384)], upstream[...]
        ).astype(LOW)
        return carry

    lax.fori_loop(0, hidden // 384, shrink_grad, 0)
    write(stage_shrink, shrink_grad_out, 10)

    def expand_grad(i, carry):
        at = pl.multiple_of(i * 256, 256)
        for part in range(3):
            cols = slice(part * block, (part + 1) * block)
            stage_expand[pl.ds(at, 256), cols] = t_dot(
                normed_two[:, pl.ds(at, 256)], pre_grad[:, cols]
            ).astype(LOW)
        return carry

    lax.fori_loop(0, width // 256, expand_grad, 0)
    write(stage_expand, expand_grad_out, 11)
    for copy in writes[2:3]:
        copy.wait()
    project_stage = triple.at[:, pl.ds(0, width)]

    def project_grad(i, carry):
        at = pl.multiple_of(i * 256, 256)
        project_stage[pl.ds(at, 256), :] = t_dot(context[:, pl.ds(at, 256)], branch[...]).astype(LOW)
        return carry

    lax.fori_loop(0, width // 256, project_grad, 0)
    write(project_stage, project_grad_out, 12)
    for i, copy in enumerate(writes):
        if i not in (2, 5):
            copy.wait()


def run_forward(fsdp, dp, counts, inputs, cotangent, packed, triple, project, expand, shrink):
    grid = Grid(fsdp, dp)
    pairs, length, width = inputs.shape
    hidden = expand.shape[1]
    rows = pairs * PAD
    hbm = pl.BlockSpec(memory_space=pltpu.HBM)
    vmem = pl.BlockSpec(memory_space=pltpu.VMEM)
    count = Gather.count(grid)
    shape = jax.ShapeDtypeStruct
    outs = [
        shape((pairs, length, width), LOW),
        shape((rows, width), LOW),
        shape((rows, 3 * width), LOW),
        shape((rows, width), LOW),
        shape((rows, width), WIDE),
        shape((rows, width), WIDE),
        shape((rows, width), LOW),
        shape((width, 3 * width), LOW),
        shape((16, width), WIDE),
        shape((8, hidden), WIDE),
        shape((hidden, width), LOW),
        shape((width, hidden), LOW),
        shape((width, width), LOW),
    ]
    scratch = [
        pltpu.VMEM((fsdp * 8, 768), LOW),
        pltpu.VMEM((width, 3 * width), LOW),
        pltpu.VMEM((width, width), LOW),
        pltpu.VMEM((width, hidden), LOW),
        pltpu.VMEM((hidden, width), LOW),
        pltpu.VMEM((16, width), WIDE),
        pltpu.VMEM((8, hidden), WIDE),
        pltpu.VMEM((rows, width), LOW),
        pltpu.VMEM((rows, 3 * width), LOW),
        pltpu.VMEM((rows, width), LOW),
        pltpu.VMEM((rows, width), WIDE),
        pltpu.VMEM((rows, width), LOW),
        pltpu.VMEM((rows, width), LOW),
        pltpu.VMEM((rows, width), LOW),
        pltpu.VMEM((rows, hidden), LOW),
        pltpu.VMEM((rows, hidden), LOW),
        pltpu.VMEM((pairs, length, width), LOW),
        pltpu.VMEM((rows, width), LOW),
        pltpu.SemaphoreType.DMA((9, count)),
        pltpu.SemaphoreType.DMA((9, count)),
        pltpu.SemaphoreType.DMA((5,)),
        pltpu.SemaphoreType.DMA((13,)),
    ]
    return pl.pallas_call(
        functools.partial(forward_kernel, grid, (pairs, length, width, hidden)),
        out_shape=outs,
        in_specs=[pl.BlockSpec(memory_space=pltpu.SMEM), vmem, vmem] + [hbm] * 5,
        out_specs=[hbm] * len(outs),
        scratch_shapes=scratch,
        compiler_params=pltpu.CompilerParams(
            collective_id=0, has_side_effects=True, vmem_limit_bytes=63 * 1024 * 1024
        ),
        name="forward_and_feed_back",
    )(counts, inputs, cotangent, packed, triple, project, expand, shrink)


def pack_small(fsdp, rows, heads, hidden, packed):
    lane = lax.broadcasted_iota(jnp.int32, (8, 768), 1)
    line = lax.broadcasted_iota(jnp.int32, (8, 768), 0)
    for f in range(fsdp):

        def turned(value, start):
            return pltpu.roll(value, 768 - start, 1) if start else value

        def piece(values, length):
            start = f * length // fsdp
            return jnp.where(
                lane < length // fsdp, turned(values[start // 768], start % 768), 0.0
            )

        wide = [jnp.broadcast_to(item, (8, 768)) for item in heads]
        deep = [jnp.broadcast_to(item, (8, 768)) for item in hidden]
        total = jnp.where(line == 2, piece(wide, 1536), piece([rows], 768))
        packed[f] = jnp.where(line == 6, piece(deep, 3072), total).astype(LOW)


def attend_back(keep_bias, qkv, context, context_grad, lse, base, width):
    first = lax.broadcasted_iota(jnp.int32, (1, 128), 1) < 64

    def heads(step, carry):
        at = pl.multiple_of(step * 128, 128)
        rows = pl.ds(base, PAD)
        query = qkv[rows, pl.ds(at, 128)] * LOW(0.125)
        key = qkv[rows, pl.ds(at + width, 128)]
        value = qkv[rows, pl.ds(at + 2 * width, 128)]
        grad = context_grad[rows, pl.ds(at, 128)]
        weighed = grad.astype(WIDE) * context[rows, pl.ds(at, 128)].astype(WIDE)
        row_lse = lse[rows, pl.ds(at, 128)]
        query_grad = jnp.zeros((PAD, 128), WIDE)
        key_grad = jnp.zeros((PAD, 128), WIDE)
        value_grad = jnp.zeros((PAD, 128), WIDE)
        for head in range(2):
            chosen = first if head == 0 else ~first
            own_query = jnp.where(chosen, query, LOW(0))
            own_key = jnp.where(chosen, key, LOW(0))
            own_grad = jnp.where(chosen, grad, LOW(0))
            scores = dot_t(own_query, key) + keep_bias
            probs = jnp.exp(scores - row_lse[:, 64 * head : 64 * head + 1])
            shift = jnp.sum(jnp.where(chosen, weighed, 0.0), axis=-1, keepdims=True)
            score_grad = (probs * (dot_t(own_grad, value) - shift)).astype(LOW)
            value_grad += t_dot(probs.astype(LOW), own_grad)
            key_grad += t_dot(score_grad, own_query)
            query_grad += dot(score_grad, own_key)
        qkv[rows, pl.ds(at, 128)] = (query_grad * 0.125).astype(LOW)
        qkv[rows, pl.ds(at + width, 128)] = key_grad.astype(LOW)
        qkv[rows, pl.ds(at + 2 * width, 128)] = value_grad.astype(LOW)
        return carry

    return heads


def backward_kernel(grid, sizes, plan, counts, *refs):
    pairs, length, width, hidden = sizes
    (
        inputs,
        vectors,
        sums,
        normed_in,
        qkv_in,
        context_in,
        lse_in,
        middle_grad_in,
        context_grad_in,
        triple_in,
        shrink_grad,
        expand_grad,
        project_grad,
        input_grad_out,
        shrink_out,
        expand_out,
        project_out,
        triple_out,
        small_out,
        normed,
        qkv,
        context,
        lse,
        middle_grad,
        context_grad,
        triple,
        triple_grad,
        packed,
        totals,
        stage_in,
    ) = refs[:30]
    n = len(plan)
    bufs = refs[30 : 30 + 10 * n]
    send, recv, local, in_sem, out_sem = refs[30 + 10 * n :]
    g = grid.locate()
    loads = []
    for index, (src, dst) in enumerate(
        (
            (qkv_in, qkv),
            (context_in, context),
            (context_grad_in, context_grad),
            (lse_in, lse),
            (normed_in, normed),
            (middle_grad_in, middle_grad),
            (triple_in, triple),
        )
    ):
        load = pltpu.make_async_copy(src, dst, in_sem.at[index])
        load.start()
        loads.append(load)
    grid.greet()
    triple_view = triple_grad.reshape(grid.F, width // grid.F, 3 * width)
    sources = (shrink_grad, expand_grad, project_grad, triple_view, packed)
    outs = (shrink_out, expand_out, project_out, triple_out, small_out)
    chunks = [
        Scatter(
            grid,
            sources[which],
            outs[which],
            pl.ds(row, rows),
            col,
            span,
            span // 6,
            bufs[10 * i : 10 * i + 10],
            send.at[i],
            recv.at[i],
            local.at[i],
        )
        for i, (which, row, rows, col, span) in enumerate(plan)
    ]
    stages = ["begin", "over_x", "over_y", "over_z", "over_pair", "over_core", "finish"]
    done = [0] * n

    def turn(step, ready):
        for i in range(n):
            if i < ready and done[i] < len(stages) and step - i >= done[i]:
                getattr(chunks[i], stages[done[i]])()
                done[i] += 1

    early = n - 4
    turn(0, early)
    turn(1, early)
    step = 2
    totals[...] = jnp.zeros_like(totals)
    for load in loads[:4]:
        load.wait()
    for b in range(pairs):
        base = b * PAD
        limit = TEXT + counts[b]
        keep = lax.broadcasted_iota(jnp.int32, (1, PAD), 1) < limit
        body = attend_back(
            jnp.where(keep, 0.0, -1e30), qkv, context, context_grad, lse, base, width
        )
        half = width // 256
        lax.fori_loop(0, half, body, 0)
        turn(step, early)
        lax.fori_loop(half, width // 128, body, 0)
        turn(step + 1, early)
        step += 2
    loads[4].wait()
    ready = early
    step = max(step, ready)
    for part in range(3):
        cols = pl.ds(part * width, width)

        def weight_grad(i, carry):
            at = pl.multiple_of(i * 256, 256)
            triple_grad[pl.ds(at, 256), cols] = t_dot(normed[:, pl.ds(at, 256)], qkv[:, cols]).astype(LOW)
            return carry

        lax.fori_loop(0, width // 256, weight_grad, 0)
        ready += 1
        turn(step, ready)
        step += 1
    loads[5].wait()
    loads[6].wait()

    def norm_grad(b, carry):
        at = pl.multiple_of(b * PAD, 32)
        rows = pl.ds(at, PAD)
        grad = dot_t(qkv[rows, :], triple[...])
        value, scale = centre(padded_rows(inputs[b], length))
        total = middle_grad[rows, :] + norm_back(grad, value, scale, vectors[0:1, :])
        stage_in[b] = total[:length].astype(LOW)
        totals[0:1, :] += jnp.sum(grad * value, axis=0, keepdims=True)
        totals[1:2, :] += jnp.sum(grad, axis=0, keepdims=True)
        for row, part in ((2, 0), (3, 2)):
            cols = pl.ds(part * width, width)
            totals[row : row + 1, :] += jnp.sum(
                qkv[rows, cols].astype(WIDE), axis=0, keepdims=True
            )
        return carry

    for b in range(pairs):
        norm_grad(b, 0)
        if b < pairs - 1:
            turn(step, ready)
            step += 1
    write = pltpu.make_async_copy(stage_in, input_grad_out, out_sem.at[0])
    write.start()
    zero = jnp.zeros((1, width), WIDE)
    lines = [
        totals[0:1, :],
        totals[1:2, :],
        zero,
        sums[2:3, 0:width],
        sums[3:4, 0:width],
        sums[4:5, 0:width],
        zero,
        sums[1:2, 0:width],
    ]
    pack_small(
        grid.F,
        jnp.concatenate(lines, axis=0),
        [totals[2:3, :], totals[3:4, :]],
        [sums[0:1, 768 * i : 768 * i + 768] for i in range(4)],
        packed,
    )
    ready += 1
    while min(done) < len(stages):
        turn(step, ready)
        step += 1
    for chunk in chunks:
        chunk.drain()
    write.wait()


def run_backward(fsdp, dp, counts, inputs, vectors, sums, kept, grads):
    grid = Grid(fsdp, dp)
    pairs, length, width = inputs.shape
    hidden = sums.shape[1]
    rows = pairs * PAD
    hbm = pl.BlockSpec(memory_space=pltpu.HBM)
    vmem = pl.BlockSpec(memory_space=pltpu.VMEM)
    shape = jax.ShapeDtypeStruct
    depth = width // fsdp
    plan = [(0, i * depth, depth, 0, width) for i in range(hidden // width)]
    plan += [(1, 0, depth, i * 768, 768) for i in range(hidden // 768)]
    plan += [(2, 0, depth, 0, width)]
    plan += [(3, 0, depth, i * width, width) for i in range(3)]
    plan += [(4, 0, 8, 0, 768)]
    count = Scatter.count(grid)
    outs = [
        shape((pairs, length, width), LOW),
        shape((hidden // fsdp, width), LOW),
        shape((depth, hidden), LOW),
        shape((depth, width), LOW),
        shape((depth, 3 * width), LOW),
        shape((8, 768), LOW),
    ]
    scratch = [
        pltpu.VMEM((rows, width), LOW),
        pltpu.VMEM((rows, 3 * width), LOW),
        pltpu.VMEM((rows, width), LOW),
        pltpu.VMEM((rows, width), WIDE),
        pltpu.VMEM((rows, width), WIDE),
        pltpu.VMEM((rows, width), LOW),
        pltpu.VMEM((width, 3 * width), LOW),
        pltpu.VMEM((width, 3 * width), LOW),
        pltpu.VMEM((fsdp, 8, 768), LOW),
        pltpu.VMEM((8, width), WIDE),
        pltpu.VMEM((pairs, length, width), LOW),
    ]
    for _, _, high, _, span in plan:
        scratch += Scatter.buffers(grid, high, span, span // 6)
    scratch += [
        pltpu.SemaphoreType.DMA((len(plan), count)),
        pltpu.SemaphoreType.DMA((len(plan), count)),
        pltpu.SemaphoreType.DMA((len(plan),)),
        pltpu.SemaphoreType.DMA((7,)),
        pltpu.SemaphoreType.DMA((1,)),
    ]
    return pl.pallas_call(
        functools.partial(backward_kernel, grid, (pairs, length, width, hidden), plan),
        out_shape=outs,
        in_specs=[pl.BlockSpec(memory_space=pltpu.SMEM), vmem, vmem, vmem] + [hbm] * 10,
        out_specs=[hbm] + [vmem] * 5,
        scratch_shapes=scratch,
        compiler_params=pltpu.CompilerParams(
            collective_id=1, has_side_effects=True, vmem_limit_bytes=63 * 1024 * 1024
        ),
        name="attention_back",
    )(counts, inputs, vectors, sums, *kept, *grads)


def shards(
    inputs,
    patch_count,
    cotangent,
    first_gain,
    first_shift,
    triple_weight,
    head_bias,
    output_weight,
    output_bias,
    second_gain,
    second_shift,
    expand_weight,
    expand_bias,
    reduce_weight,
    reduce_bias,
):
    fsdp, dp = lax.axis_size("fsdp"), lax.axis_size("dp")
    small = (
        first_gain,
        first_shift,
        head_bias,
        output_bias,
        second_gain,
        second_shift,
        expand_bias,
        reduce_bias,
    )
    packed = jnp.stack([jnp.pad(item, (0, 768 - item.shape[0])) for item in small])
    (
        layer_output,
        hidden_one,
        triple_rows,
        context,
        lse,
        middle_grad,
        context_grad,
        triple,
        vectors,
        sums,
        shrink_grad,
        expand_grad,
        project_grad,
    ) = run_forward(
        fsdp,
        dp,
        patch_count,
        inputs,
        cotangent,
        packed,
        triple_weight,
        output_weight,
        expand_weight,
        reduce_weight,
    )
    grads = tuple(
        item.reshape(fsdp, -1, item.shape[-1]) for item in (shrink_grad, expand_grad, project_grad)
    )
    input_gradient, *shares, small_sums = run_backward(
        fsdp,
        dp,
        patch_count,
        inputs,
        vectors,
        sums,
        (hidden_one, triple_rows, context, lse, middle_grad, context_grad, triple),
        grads,
    )
    shrink_sum, expand_sum, project_sum, triple_sum = (item.astype(WIDE) for item in shares)
    (
        gain_one_sum,
        shift_one_sum,
        head_bias_sum,
        project_bias_sum,
        gain_two_sum,
        shift_two_sum,
        expand_add_sum,
        shrink_add_sum,
    ) = (small_sums[index, : item.shape[0]].astype(WIDE) for index, item in enumerate(small))
    return (
        layer_output,
        input_gradient,
        gain_one_sum,
        shift_one_sum,
        triple_sum,
        head_bias_sum,
        project_sum,
        project_bias_sum,
        gain_two_sum,
        shift_two_sum,
        expand_sum,
        expand_add_sum,
        shrink_sum,
        shrink_add_sum,
    )


def solution(mesh):
    in_specs = (
        P(("dp", "fsdp"), None, None),
        P(("dp", "fsdp")),
        P(("dp", "fsdp"), None, None),
        P("fsdp"),
        P("fsdp"),
        P("fsdp", None),
        P("fsdp"),
        P("fsdp", None),
        P("fsdp"),
        P("fsdp"),
        P("fsdp"),
        P("fsdp", None),
        P("fsdp"),
        P("fsdp", None),
        P("fsdp"),
    )
    out_specs = (
        P(("dp", "fsdp"), None, None),
        P(("dp", "fsdp"), None, None),
        P("fsdp"),
        P("fsdp"),
        P("fsdp", None),
        P("fsdp"),
        P("fsdp", None),
        P("fsdp"),
        P("fsdp"),
        P("fsdp"),
        P("fsdp", None),
        P("fsdp"),
        P("fsdp", None),
        P("fsdp"),
    )
    return jax.shard_map(shards, mesh=mesh, in_specs=in_specs, out_specs=out_specs, check_vma=False)
```

```python
import functools

import jax
import jax.numpy as jnp
from jax import lax
from jax.experimental import pallas as pl
from jax.experimental.pallas import tpu as pltpu
from jax.sharding import PartitionSpec as P

TEXT = 40
MESH = pl.DeviceIdType.MESH


class Grid:
    def __init__(self, fsdp, dp):
        self.H = dp // 4
        y_size = 1
        while y_size * y_size * 8 <= fsdp:
            y_size *= 2
        self.F, self.Y, self.Z = fsdp, y_size, fsdp // y_size

    def locate(self):
        self.dp = lax.axis_index("dp")
        self.f = lax.axis_index("fsdp")
        self.c = lax.rem(self.dp, 2)
        self.x = lax.rem(self.dp // 2, 2)
        self.h = self.dp // 4
        self.z = self.f // self.Y
        self.y = lax.rem(self.f, self.Y)
        return self

    def core_peer(self):
        return (self.dp + 1 - 2 * self.c, self.f)

    def x_peer(self):
        return (self.dp + 2 - 4 * self.x, self.f)

    def far_index(self, dh):
        return lax.rem(self.h + self.H + dh, self.H)

    def far_peer(self, dh):
        return (self.far_index(dh) * 4 + lax.rem(self.dp, 4), self.f)

    def z_index(self, dz):
        return lax.rem(self.z + self.Z + dz, self.Z)

    def y_index(self, dy):
        return lax.rem(self.y + self.Y + dy, self.Y)

    def z_peer(self, dz):
        return (self.dp, self.z_index(dz) * self.Y + self.y)

    def y_peer(self, dy):
        return (self.dp, self.z * self.Y + self.y_index(dy))

    def source(self, dz, dy):
        return self.z_index(-dz) * self.Y + self.y_index(-dy)

    def greet(self):
        barrier = pltpu.get_barrier_semaphore()
        peers = [self.core_peer(), self.x_peer()]
        peers += [self.z_peer(dz) for dz in range(1, self.Z)]
        peers += [self.y_peer(dy) for dy in range(1, self.Y)]
        peers += [self.far_peer(dh) for dh in range(1, self.H)]
        for peer in peers:
            pl.semaphore_signal(barrier, inc=1, device_id=peer, device_id_type=MESH)
        pl.semaphore_wait(barrier, len(peers))


def remote(src, dst, send, recv, peer):
    return pltpu.make_async_remote_copy(
        src_ref=src,
        dst_ref=dst,
        send_sem=send,
        recv_sem=recv,
        device_id=peer,
        device_id_type=MESH,
    )


def lanes(start, width):
    return pl.ds(pl.multiple_of(start, 128), width)


class Gather:
    def __init__(self, grid, src, dst, depth, row, rows, col, width, send, recv):
        self.g, self.src, self.dst = grid, src, dst
        self.depth, self.row, self.rows = depth, row, rows
        self.send, self.recv = send, recv
        half, group = width // 2, width // 6
        self.sent = []
        g = grid
        self.mine = lanes(col + g.c * half + g.x * group, 2 * group)
        self.x_out = lanes(col + g.c * half + 2 * g.x * group, group)
        self.x_in = lanes(col + g.c * half + 2 * (1 - g.x) * group, group)
        self.core_out = lanes(col + g.c * half, half)
        self.core_in = lanes(col + (1 - g.c) * half, half)
        self.z_base, self.y_base = 0, g.Z - 1
        self.x_base = self.y_base + g.Z * (g.Y - 1)
        self.c_base = self.x_base + g.F - 1

    @staticmethod
    def count(grid):
        return grid.Z - 1 + grid.Z * (grid.Y - 1) + 2 * (grid.F - 1)

    def view(self, shard, columns):
        start = pl.multiple_of(shard * self.depth + self.row, 8)
        return self.dst.at[pl.ds(start, self.rows), columns]

    def push(self, src, dst, index, peer):
        copy = remote(src, dst, self.send.at[index], self.recv.at[index], peer)
        copy.start()
        self.sent.append(copy)

    def arrive(self, view, index):
        pltpu.make_async_copy(view, view, self.recv.at[index]).wait()

    def pairs(self):
        return [(dz, dy) for dy in range(self.g.Y) for dz in range(self.g.Z) if dz + dy > 0]

    def slot(self, dz, dy):
        return dz * self.g.Y + dy - 1

    def begin(self):
        g = self.g
        own = self.src.at[pl.ds(self.row, self.rows), self.mine]
        for dz in range(1, g.Z):
            self.push(own, self.view(g.f, self.mine), self.z_base + dz - 1, g.z_peer(dz))
        for dy in range(1, g.Y):
            self.push(own, self.view(g.f, self.mine), self.y_base + dy - 1, g.y_peer(dy))

    def over_y(self):
        g = self.g
        for dz in range(1, g.Z):
            shard = g.source(dz, 0)
            self.arrive(self.view(shard, self.mine), self.z_base + dz - 1)
            for dy in range(1, g.Y):
                self.push(
                    self.view(shard, self.mine),
                    self.view(shard, self.mine),
                    self.y_base + dz * (g.Y - 1) + dy - 1,
                    g.y_peer(dy),
                )
            self.over_x(dz, 0)

    def over_x(self, dz, dy):
        g = self.g
        view = self.view(g.source(dz, dy), self.x_out)
        self.push(view, view, self.x_base + self.slot(dz, dy), g.x_peer())

    def finish_y(self):
        g = self.g
        for dz in range(g.Z):
            for dy in range(1, g.Y):
                shard = g.source(dz, dy)
                self.arrive(self.view(shard, self.mine), self.y_base + dz * (g.Y - 1) + dy - 1)
                self.over_x(dz, dy)

    def over_core(self):
        g = self.g
        for dz, dy in self.pairs():
            shard = g.source(dz, dy)
            self.arrive(self.view(shard, self.x_in), self.x_base + self.slot(dz, dy))
            view = self.view(shard, self.core_out)
            self.push(view, view, self.c_base + self.slot(dz, dy), g.core_peer())

    def finish(self):
        g = self.g
        for dz, dy in self.pairs():
            shard = g.source(dz, dy)
            self.arrive(self.view(shard, self.core_in), self.c_base + self.slot(dz, dy))

    def drain(self):
        for copy in self.sent:
            copy.wait_send()


class Scatter:
    WAITS = {"begin": -1, "over_x": 1, "over_y": 3, "over_z": 5, "over_pair": 7, "over_core": 9, "finish": 10}

    def __init__(self, grid, whole, part, out, rows, width, bufs, send, recv, leave, before):
        g = self.g = grid
        self.leave, self.before, self.leaving = leave, before, []
        self.whole, self.part, self.out, self.rows = whole, part, out, rows
        self.send, self.recv = send, recv
        half, apart = width // 2, width // 6
        self.apart, self.shared = apart, half - 2 * apart
        keep, give = g.c * half, (1 - g.c) * half
        self.core_keep, self.core_give = lanes(keep, half), lanes(give, half)
        far_x, near_x = (1 - g.x) * (half - apart), g.x * (half - apart)
        self.x_keep, self.x_give = lanes(keep + near_x, apart), lanes(keep + far_x, apart)
        self.x_own, self.x_other = lanes(near_x, apart), lanes(far_x, apart)
        self.kept = lanes(keep + g.x * apart, half - apart)
        self.core_in, self.x_in, self.y_in, self.z_sum, self.z_in, self.f_out, self.f_in, self.e_out, self.far = bufs
        self.todo = list(self.WAITS)
        self.sent = []

    @staticmethod
    def buffers(grid, rows, width):
        half = width // 2
        part = half - width // 6
        shapes = [
            (grid.F, rows, half),
            (grid.F, rows, width // 6),
            ((grid.Y - 1) * grid.Z, rows, part),
            (grid.Z, rows, part),
            (grid.Z - 1, rows, part),
            (rows, part),
            (rows, part),
            (2, rows, half),
            (grid.H, rows, part),
        ]
        return [pltpu.VMEM(shape, jnp.bfloat16) for shape in shapes]

    @staticmethod
    def count(grid):
        return 4 + grid.Z * (grid.Y - 1) + grid.Z - 1 + grid.H - 1

    def push(self, src, dst, index, peer):
        copy = remote(src, dst, self.send.at[index], self.recv.at[index], peer)
        copy.start()
        self.sent.append(copy)

    def settle(self):
        for copy in self.sent:
            copy.wait()
        self.sent = []

    def begin(self):
        source = self.whole(self.core_give)
        target = self.core_in
        if len(source.shape) == 2:
            target = target.reshape(source.shape)
        self.push(source, target, 0, self.g.core_peer())

    def each(self, count, body):
        def step(i, carry):
            body(i)
            return carry

        lax.fori_loop(0, count, step, 0)

    def over_x(self):
        self.settle()

        def body(i):
            view = self.part(i, self.core_keep)
            view[...] = plus(view[...], self.core_in[i])

        self.each(self.g.F, body)
        source = self.whole(self.x_give)
        target = self.x_in
        if len(source.shape) == 2:
            target = target.reshape(source.shape)
        self.push(source, target, 1, self.g.x_peer())

    def over_y(self):
        g = self.g
        self.settle()

        def body(i):
            view = self.part(i, self.x_keep)
            view[...] = plus(view[...], self.x_in[i])

        self.each(g.F, body)
        for dz in range(g.Z):
            for dy in range(1, g.Y):
                slot = (dy - 1) * g.Z + dz
                self.push(
                    self.part(dz * g.Y + g.y_index(dy), self.kept),
                    self.y_in.at[slot],
                    4 + slot,
                    g.y_peer(dy),
                )

    def over_z(self):
        g = self.g
        self.settle()

        def body(i):
            total = self.part(i * g.Y + g.y, self.kept)[...].astype(jnp.float32)
            for dy in range(1, g.Y):
                total += self.y_in[(dy - 1) * g.Z + i].astype(jnp.float32)
            self.z_sum[i] = total.astype(jnp.bfloat16)

        self.each(g.Z, body)
        for dz in range(1, g.Z):
            self.push(
                self.z_sum.at[g.z_index(dz)],
                self.z_in.at[dz - 1],
                4 + g.Z * (g.Y - 1) + dz - 1,
                g.z_peer(dz),
            )

    def over_pair(self):
        g = self.g
        self.settle()
        total = self.z_sum[g.z].astype(jnp.float32)
        for dz in range(1, g.Z):
            total += self.z_in[dz - 1].astype(jnp.float32)
        self.f_out[...] = total.astype(jnp.bfloat16)
        if g.H > 1:
            self.over_far()
        self.push(self.f_out, self.f_in, 2, g.x_peer())

    def over_far(self):
        g = self.g
        base = 4 + g.Z * (g.Y - 1) + g.Z - 2
        self.far[g.h] = self.f_out[...]
        for dh in range(1, g.H):
            self.push(self.f_out, self.far.at[g.h], base + dh, g.far_peer(dh))
        for dh in range(1, g.H):
            view = self.far.at[g.far_index(-dh)]
            pltpu.make_async_copy(view, view, self.recv.at[base + dh]).wait()
        for copy in self.sent:
            copy.wait_send()
        self.sent = []
        total = self.far[0].astype(jnp.float32)
        for h in range(1, g.H):
            total += self.far[h].astype(jnp.float32)
        self.f_out[...] = total.astype(jnp.bfloat16)

    def over_core(self):
        g = self.g
        self.settle()
        shared_out = lanes((1 - g.x) * self.apart, self.shared)
        shared_in = lanes(g.x * self.apart, self.shared)
        if self.before is not None:
            self.before.left()
        own = lanes(g.x * self.shared, self.apart)
        other = lanes((1 - g.x) * self.shared, self.apart)
        e = self.e_out.at[0]
        e[:, lanes(self.apart, self.shared)] = plus(self.f_out[:, shared_out], self.f_in[:, shared_in])
        e[:, self.x_own] = self.f_out[:, own]
        e[:, self.x_other] = self.f_in[:, other]
        self.push(e, self.e_out.at[1], 3, g.core_peer())

    def finish(self):
        self.settle()
        for index, columns in enumerate((self.core_keep, self.core_give)):
            copy = pltpu.make_async_copy(
                self.e_out.at[index], self.out(columns), self.leave.at[index]
            )
            copy.start()
            self.leaving.append(copy)

    def left(self):
        for copy in self.leaving:
            copy.wait()
        self.leaving = []

    def advance(self, step):
        if not self.todo or step < self.WAITS[self.todo[0]]:
            return
        if self.before is None or len(self.before.todo) <= max(len(self.todo) - 2, 0):
            getattr(self, self.todo.pop(0))()


def plus(left, right):
    return (left.astype(jnp.float32) + right.astype(jnp.float32)).astype(jnp.bfloat16)


NORM_EPSILON = 1e-06
PAD = 288
LOW = jnp.bfloat16
WIDE = jnp.float32
SMALL = ("gain_one", "shift_one", "heads", "project", "gain_two", "shift_two", "expand", "shrink")


def dot(left, right):
    return jnp.dot(left, right, preferred_element_type=WIDE)


def dot_t(left, right):
    return lax.dot_general(left, right, (((1,), (1,)), ((), ())), preferred_element_type=WIDE)


def t_dot(left, right):
    return lax.dot_general(left, right, (((0,), (0,)), ((), ())), preferred_element_type=WIDE)


def padded_rows(value, length):
    wide = value.astype(WIDE)
    if length == PAD:
        return wide
    return jnp.concatenate([wide, jnp.zeros((PAD - length, wide.shape[1]), WIDE)], axis=0)


def centre(wide):
    centred = wide - jnp.mean(wide, axis=-1, keepdims=True)
    scale = lax.rsqrt(jnp.mean(centred * centred, axis=-1, keepdims=True) + NORM_EPSILON)
    return centred * scale, scale


def norm_back(grad, normed, scale, gain):
    inner = grad * gain
    return scale * (
        inner
        - jnp.mean(inner, axis=-1, keepdims=True)
        - normed * jnp.mean(inner * normed, axis=-1, keepdims=True)
    )


def gelu_parts(value):
    bell = jnp.exp(value * value * -0.5)
    t = 1.0 / (1.0 + jnp.abs(value) * (0.3275911 * 0.7071067811865476))
    poly = t * (
        0.5 * 0.254829592
        + t
        * (
            0.5 * -0.284496736
            + t * (0.5 * 1.421413741 + t * (0.5 * -1.453152027 + t * (0.5 * 1.061405429)))
        )
    )
    tail = poly * bell
    return jnp.where(value >= 0, 1.0 - tail, tail), value * bell * 0.3989422804014327


def unpack_small(fsdp, packed, vectors):
    first = jnp.zeros((8, 768), WIDE)
    heads = [jnp.zeros((8, 768), WIDE) for _ in range(2)]
    hidden = [jnp.zeros((8, 768), WIDE) for _ in range(4)]
    for f in range(fsdp):
        rows = packed[pl.ds(8 * f, 8), :].astype(WIDE)

        def turned(length):
            start = f * length // fsdp
            return start // 768, (pltpu.roll(rows, start % 768, 1) if start % 768 else rows)

        _, value = turned(768)
        first += value
        part, value = turned(1536)
        heads[part] += value
        part, value = turned(3072)
        hidden[part] += value
    vectors[0:8, :] = first
    vectors[2:3, :] = heads[0][2:3]
    vectors[8:9, :] = heads[1][2:3]
    for part in range(4):
        vectors[9 + part : 10 + part, :] = hidden[part][6:7]


def place(step, counts, width):
    blocks = width // 128
    pair = step // blocks
    at = pl.multiple_of(lax.rem(step, blocks) * 128, 128)
    keep = lax.broadcasted_iota(jnp.int32, (1, PAD), 1) < TEXT + counts[pair]
    return pl.ds(pl.multiple_of(pair * PAD, 32), PAD), at, jnp.where(keep, 0.0, -1e30)


def attend(counts, qkv, context, lse, width):
    first = lax.broadcasted_iota(jnp.int32, (1, 128), 1) < 64

    def heads(step, carry):
        rows, at, keep_bias = place(step, counts, width)
        query = qkv[rows, pl.ds(at, 128)] * LOW(0.125)
        key = qkv[rows, pl.ds(at + width, 128)]
        value = qkv[rows, pl.ds(at + 2 * width, 128)]
        outs = []
        for head in range(2):
            chosen = first if head == 0 else ~first
            scores = dot_t(jnp.where(chosen, query, LOW(0)), key) + keep_bias
            top = jnp.max(scores, axis=-1, keepdims=True)
            expo = jnp.exp(scores - top)
            total = jnp.sum(expo, axis=-1, keepdims=True)
            outs.append((dot(expo.astype(LOW), value) * (1.0 / total), top + jnp.log(total)))
        context[rows, pl.ds(at, 128)] = jnp.where(first, outs[0][0], outs[1][0]).astype(LOW)
        lse[rows, pl.ds(at, 128)] = jnp.where(first, outs[0][1], outs[1][1])
        return carry

    return heads


def pack_small(fsdp, rows, heads, hidden, packed):
    lane = lax.broadcasted_iota(jnp.int32, (8, 768), 1)
    line = lax.broadcasted_iota(jnp.int32, (8, 768), 0)
    for f in range(fsdp):

        def turned(value, start):
            return pltpu.roll(value, 768 - start, 1) if start else value

        def piece(values, length):
            start = f * length // fsdp
            return jnp.where(
                lane < length // fsdp, turned(values[start // 768], start % 768), 0.0
            )

        wide = [jnp.broadcast_to(item, (8, 768)) for item in heads]
        deep = [jnp.broadcast_to(item, (8, 768)) for item in hidden]
        total = jnp.where(line == 2, piece(wide, 1536), piece([rows], 768))
        packed[f] = jnp.where(line == 6, piece(deep, 3072), total).astype(LOW)


def attend_back(counts, qkv, context, context_grad, lse, width):
    first = lax.broadcasted_iota(jnp.int32, (1, 128), 1) < 64

    def heads(step, carry):
        rows, at, keep_bias = place(step, counts, width)
        query = qkv[rows, pl.ds(at, 128)] * LOW(0.125)
        key = qkv[rows, pl.ds(at + width, 128)]
        value = qkv[rows, pl.ds(at + 2 * width, 128)]
        grad = context_grad[rows, pl.ds(at, 128)]
        weighed = grad.astype(WIDE) * context[rows, pl.ds(at, 128)].astype(WIDE)
        row_lse = lse[rows, pl.ds(at, 128)]
        query_grad = jnp.zeros((PAD, 128), WIDE)
        key_grad = jnp.zeros((PAD, 128), WIDE)
        value_grad = jnp.zeros((PAD, 128), WIDE)
        for head in range(2):
            chosen = first if head == 0 else ~first
            own_query = jnp.where(chosen, query, LOW(0))
            own_key = jnp.where(chosen, key, LOW(0))
            own_grad = jnp.where(chosen, grad, LOW(0))
            scores = dot_t(own_query, key) + keep_bias
            probs = jnp.exp(scores - row_lse[:, 64 * head : 64 * head + 1])
            shift = jnp.sum(jnp.where(chosen, weighed, 0.0), axis=-1, keepdims=True)
            score_grad = (probs * (dot_t(own_grad, value) - shift)).astype(LOW)
            value_grad += t_dot(probs.astype(LOW), own_grad)
            key_grad += t_dot(score_grad, own_query)
            query_grad += dot(score_grad, own_key)
        qkv[rows, pl.ds(at, 128)] = (query_grad * 0.125).astype(LOW)
        qkv[rows, pl.ds(at + width, 128)] = key_grad.astype(LOW)
        qkv[rows, pl.ds(at + 2 * width, 128)] = value_grad.astype(LOW)
        return carry

    return heads


def layer_kernel(grid, sizes, plans, counts, *refs):
    pairs, length, width, hidden = sizes
    gather_plan, scatter_plan = plans
    small_in, refs = refs[:8], refs[8:]
    (
        inputs,
        cotangent,
        triple_in,
        project_in,
        expand_in,
        shrink_in,
        layer_out,
        input_grad_out,
        shrink_out,
        expand_out,
        project_out,
        triple_out,
        small_out,
        packed_in,
        packed,
        triple,
        project,
        expand,
        shrink,
        vectors,
        sums,
        normed,
        qkv,
        context,
        lse,
        middle,
        normed_two,
        upstream,
        branch,
        context_grad,
        activated,
        pre_grad,
        stage,
        packed_grad,
    ) = refs[:34]
    last = len(refs) - 7
    bufs = refs[34:last]
    gather_send, gather_recv, scatter_send, scatter_recv, local, out_sem, leave = refs[last:]
    g = grid.locate()
    fsdp = grid.F

    packed_in[...] = jnp.zeros_like(packed_in)
    for index, item in enumerate(small_in):
        packed_in[index : index + 1, 0 : item.shape[1]] = item[...]
    sources = (packed_in, triple_in, project_in, expand_in, shrink_in)
    wholes = (packed, triple, project, expand, shrink)
    owns = []
    for index in range(5):
        depth = sources[index].shape[0]
        own = pltpu.make_async_copy(
            sources[index],
            wholes[index].at[pl.ds(pl.multiple_of(g.f * depth, 8), depth)],
            local.at[index],
        )
        own.start()
        owns.append(own)
    cotangent_load = pltpu.make_async_copy(cotangent, stage, local.at[5])
    cotangent_load.start()
    grid.greet()
    fetches = [
        Gather(
            grid,
            sources[which],
            wholes[which],
            sources[which].shape[0],
            row,
            rows,
            col,
            span,
            gather_send.at[i],
            gather_recv.at[i],
        )
        for i, (which, row, rows, col, span) in enumerate(gather_plan)
    ]
    n = len(fetches)
    urgent, ahead = 4, 4

    def fetch_turn(step):
        for i in range(n):
            skew = 1 if i < urgent else 2
            if step == i + 2 * skew:
                fetches[i].over_core()
            if step == i + skew:
                fetches[i].finish_y()
            if step == i:
                fetches[i].over_y()
            if step + ahead == i:
                fetches[i].begin()

    for i in range(ahead):
        fetches[i].begin()
    for step in range(3):
        fetch_turn(step)
    owns[0].wait()
    fetches[0].finish()
    unpack_small(fsdp, packed, vectors)
    sums[...] = jnp.zeros_like(sums)

    def vector(row, rows=1):
        return vectors[row : row + rows, :]

    def pair_rows(b):
        return pl.ds(pl.multiple_of(b * PAD, 32), PAD)

    def norm_one(b, carry):
        value, _ = centre(padded_rows(inputs[b], length))
        normed[pair_rows(b), :] = (value * vector(0) + vector(1)).astype(LOW)
        return carry

    fetch_turn(3)
    lax.fori_loop(0, pairs, norm_one, 0)
    fetch_turn(4)
    fetch_turn(5)
    owns[1].wait()
    for i in range(1, urgent):
        fetches[i].finish()

    def project_heads(b, carry):
        rows = pair_rows(b)
        for part in range(3):
            cols = pl.ds(part * width, width)
            value = dot(normed[rows, :], triple[:, cols])
            if part != 1:
                value += vector(2 if part == 0 else 8)
            qkv[rows, cols] = value.astype(LOW)
        return carry

    lax.fori_loop(0, pairs, project_heads, 0)
    step = 6
    heads = attend(counts, qkv, context, lse, width)
    steps = pairs * width // 128
    for i in range(0, steps, 3):
        lax.fori_loop(i, min(i + 3, steps), heads, 0)
        fetch_turn(step)
        step += 1
    while step < urgent + 1 + len(gather_plan[5:-4]) + 4:
        fetch_turn(step)
        step += 1
    for own in owns[2:4]:
        own.wait()
    shrink_first = n - 4
    for i in range(urgent, shrink_first):
        fetches[i].finish()

    block = hidden // 3

    def feed_in(b, carry):
        rows = pair_rows(b)
        total = padded_rows(inputs[b], length) + dot(context[rows, :], project[...]) + vector(3)
        middle[rows, :] = total
        value, _ = centre(total)
        second = (value * vector(4) + vector(5)).astype(LOW)
        normed_two[rows, :] = second
        for part in range(3):
            cols = slice(part * block, (part + 1) * block)
            bias = jnp.concatenate([vector(9 + i) for i in range(4)], axis=1)[:, cols]
            pre = dot(second, expand[:, cols]) + bias
            share, slope = gelu_parts(pre)
            activated[rows, cols] = (pre * share).astype(LOW)
            pre_grad[rows, cols] = (share + slope).astype(LOW)
        return carry

    for b in range(0, pairs, 2):
        lax.fori_loop(b, min(b + 2, pairs), feed_in, 0)
        for _ in range(2):
            if step < n + 4:
                fetch_turn(step)
                step += 1
    while step < n + 4:
        fetch_turn(step)
        step += 1
    owns[4].wait()
    for i in range(shrink_first, n):
        fetches[i].finish()
    cotangent_load.wait()

    def feed_out(b, carry):
        rows = pair_rows(b)
        valid = lax.broadcasted_iota(jnp.int32, (PAD, 1), 0) < TEXT + counts[b]
        above = jnp.where(valid, padded_rows(stage[b], length), 0.0)
        above_low = above.astype(LOW)
        upstream[rows, :] = above_low
        mixed = jnp.zeros((PAD, width), WIDE)
        back = jnp.zeros((PAD, width), WIDE)
        for part in range(3):
            cols = slice(part * block, (part + 1) * block)
            act_grad = dot_t(above_low, shrink[cols, :])
            grad = (act_grad * pre_grad[rows, cols].astype(WIDE)).astype(LOW)
            pre_grad[rows, cols] = grad
            mixed += dot(activated[rows, cols], shrink[cols, :])
            back += dot_t(grad, expand[:, cols])
            sums[0:1, cols] += jnp.sum(grad.astype(WIDE), axis=0, keepdims=True)
        total = middle[rows, :]
        layer = jnp.where(valid, total + mixed + vector(7), 0.0)
        stage[b] = layer[:length].astype(LOW)
        value, scale = centre(total)
        middle_grad = above + norm_back(back, value, scale, vector(4))
        middle[rows, :] = middle_grad
        low_grad = middle_grad.astype(LOW)
        branch[rows, :] = low_grad
        context_grad[rows, :] = dot_t(low_grad, project[...]).astype(LOW)
        for row, term in (
            (1, above),
            (2, low_grad.astype(WIDE)),
            (3, back * value),
            (4, back),
        ):
            sums[row : row + 1, 0:width] += jnp.sum(term, axis=0, keepdims=True)
        return carry

    lax.fori_loop(0, pairs, feed_out, 0)
    layer_write = pltpu.make_async_copy(stage, layer_out, out_sem.at[0])
    layer_write.start()
    for fetch in fetches:
        fetch.drain()

    depth = width // fsdp
    shrink_view = shrink.reshape(fsdp, hidden // fsdp, width)
    outs = (shrink_out, expand_out, project_out, triple_out, small_out)

    def views(which, row, rows, col, span):
        def at(columns):
            return lanes(columns.start + col, columns.size)

        if which == 0:
            whole = lambda columns: shrink_view.at[:, pl.ds(row, rows), at(columns)]
            part = lambda i, columns: shrink_view.at[i, pl.ds(row, rows), at(columns)]
        elif which == 4:
            whole = lambda columns: packed_grad.at[:, :, at(columns)]
            part = lambda i, columns: packed_grad.at[i, :, at(columns)]
        else:
            source = (None, expand, project, pre_grad)[which]
            whole = lambda columns: source.at[pl.ds(0, width), at(columns)]
            part = lambda i, columns: source.at[
                pl.ds(pl.multiple_of(i * depth, 8), depth), at(columns)
            ]
        out = lambda columns: outs[which].at[pl.ds(row, rows), at(columns)]
        return whole, part, out

    sets = 4
    per_set = 9
    shares = []
    for i, (which, row, rows, col, span) in enumerate(scatter_plan):
        whole, part, out = views(which, row, rows, col, span)
        at = (i % sets if which != 4 else sets) * per_set
        shares.append(
            Scatter(
                grid,
                whole,
                part,
                out,
                rows,
                span,
                bufs[at : at + per_set],
                scatter_send.at[i],
                scatter_recv.at[i],
                leave.at[i],
                shares[i - 2] if i > 1 else None,
            )
        )
    ready, turns = [0], [-1]

    def share_turn(more=0):
        ready[0] += more
        turns[0] += 1
        for i in range(ready[0]):
            shares[i].advance(turns[0] - i)

    for col in range(0, hidden, width):

        def expand_grad(i, carry):
            at = pl.multiple_of(i * 256, 256)
            expand[pl.ds(at, 256), pl.ds(col, width)] = t_dot(
                normed_two[:, pl.ds(at, 256)], pre_grad[:, pl.ds(col, width)]
            ).astype(LOW)
            return carry

        lax.fori_loop(0, width // 256, expand_grad, 0)
        share_turn(1)

    def project_grad(i, carry):
        at = pl.multiple_of(i * 256, 256)
        project[pl.ds(at, 256), :] = t_dot(context[:, pl.ds(at, 256)], branch[...]).astype(LOW)
        return carry

    lax.fori_loop(0, width // 256, project_grad, 0)
    share_turn(1)

    def shrink_grad(i, carry):
        at = pl.multiple_of(i * 384, 384)
        shrink[pl.ds(at, 384), :] = t_dot(activated[:, pl.ds(at, 384)], upstream[...]).astype(LOW)
        return carry

    lax.fori_loop(0, hidden // 768, shrink_grad, 0)
    share_turn()
    lax.fori_loop(hidden // 768, hidden // 384, shrink_grad, 0)
    share_turn(hidden // width)
    heads_back = attend_back(counts, qkv, context, context_grad, lse, width)
    for i in range(0, steps, 4):
        lax.fori_loop(i, min(i + 4, steps), heads_back, 0)
        share_turn()
    for part in range(3):
        cols = pl.ds(part * width, width)

        def weight_grad(i, carry):
            at = pl.multiple_of(i * 256, 256)
            pre_grad[pl.ds(at, 256), cols] = t_dot(normed[:, pl.ds(at, 256)], qkv[:, cols]).astype(LOW)
            return carry

        lax.fori_loop(0, width // 256, weight_grad, 0)
        share_turn(1)
    layer_write.wait()
    totals = vectors.at[pl.ds(8, 8)]
    totals[...] = jnp.zeros_like(totals)

    def norm_grad(b, carry):
        rows = pair_rows(b)
        grad = dot_t(qkv[rows, :], triple[...])
        value, scale = centre(padded_rows(inputs[b], length))
        total = middle[rows, :] + norm_back(grad, value, scale, vector(0))
        stage[b] = total[:length].astype(LOW)
        totals[0:1, :] += jnp.sum(grad * value, axis=0, keepdims=True)
        totals[1:2, :] += jnp.sum(grad, axis=0, keepdims=True)
        for row, part in ((2, 0), (3, 2)):
            cols = pl.ds(part * width, width)
            totals[row : row + 1, :] += jnp.sum(
                qkv[rows, cols].astype(WIDE), axis=0, keepdims=True
            )
        return carry

    for b in range(0, pairs, 2):
        lax.fori_loop(b, min(b + 2, pairs), norm_grad, 0)
        if b + 2 < pairs:
            share_turn()
    write = pltpu.make_async_copy(stage, input_grad_out, out_sem.at[1])
    write.start()
    zero = jnp.zeros((1, width), WIDE)
    lines = [
        totals[0:1, :],
        totals[1:2, :],
        zero,
        sums[2:3, 0:width],
        sums[3:4, 0:width],
        sums[4:5, 0:width],
        zero,
        sums[1:2, 0:width],
    ]
    pack_small(
        fsdp,
        jnp.concatenate(lines, axis=0),
        [totals[2:3, :], totals[3:4, :]],
        [sums[0:1, 768 * i : 768 * i + 768] for i in range(4)],
        packed_grad,
    )
    share_turn(1)
    while any(share.todo for share in shares):
        share_turn()
    for share in shares:
        share.left()
    write.wait()


def run_layer(fsdp, dp, counts, small, inputs, cotangent, triple, project, expand, shrink):
    grid = Grid(fsdp, dp)
    pairs, length, width = inputs.shape
    hidden = expand.shape[1]
    rows = pairs * PAD
    depth = width // fsdp
    hbm = pl.BlockSpec(memory_space=pltpu.HBM)
    vmem = pl.BlockSpec(memory_space=pltpu.VMEM)
    shape = jax.ShapeDtypeStruct
    gather_plan = [(0, 0, 8, 0, 768)]
    gather_plan += [(1, 0, depth, col, 768) for col in range(0, 3 * width, 768)]
    gather_plan += [(2, 0, depth, 0, width)]
    gather_plan += [(3, 0, depth, col, 768) for col in range(0, hidden, 768)]
    gather_plan += [(4, row, depth, 0, width) for row in range(0, hidden // fsdp, depth)]
    scatter_plan = [(1, 0, depth, i * 768, 768) for i in range(hidden // 768)]
    scatter_plan += [(2, 0, depth, 0, width)]
    scatter_plan += [(0, i * depth, depth, 0, width) for i in range(hidden // width)]
    scatter_plan += [(3, 0, depth, i * width, width) for i in range(3)]
    scatter_plan += [(4, 0, 8, 0, 768)]
    outs = [
        shape((pairs, length, width), LOW),
        shape((pairs, length, width), LOW),
        shape((hidden // fsdp, width), LOW),
        shape((depth, hidden), LOW),
        shape((depth, width), LOW),
        shape((depth, 3 * width), LOW),
        shape((8, 768), LOW),
    ]
    scratch = [
        pltpu.VMEM((8, 768), LOW),
        pltpu.VMEM((fsdp * 8, 768), LOW),
        pltpu.VMEM((width, 3 * width), LOW),
        pltpu.VMEM((width, width), LOW),
        pltpu.VMEM((width, hidden), LOW),
        pltpu.VMEM((hidden, width), LOW),
        pltpu.VMEM((16, width), WIDE),
        pltpu.VMEM((8, hidden), WIDE),
        pltpu.VMEM((rows, width), LOW),
        pltpu.VMEM((rows, 3 * width), LOW),
        pltpu.VMEM((rows, width), LOW),
        pltpu.VMEM((rows, width), WIDE),
        pltpu.VMEM((rows, width), WIDE),
        pltpu.VMEM((rows, width), LOW),
        pltpu.VMEM((rows, width), LOW),
        pltpu.VMEM((rows, width), LOW),
        pltpu.VMEM((rows, width), LOW),
        pltpu.VMEM((rows, hidden), LOW),
        pltpu.VMEM((rows, hidden), LOW),
        pltpu.VMEM((pairs, length, width), LOW),
        pltpu.VMEM((fsdp, 8, 768), LOW),
    ]
    for _ in range(4):
        scratch += Scatter.buffers(grid, depth, 768)
    scratch += Scatter.buffers(grid, 8, 768)
    for plan, count in ((gather_plan, Gather.count(grid)), (scatter_plan, Scatter.count(grid))):
        scratch += [pltpu.SemaphoreType.DMA((len(plan), count))] * 2
    scratch += [pltpu.SemaphoreType.DMA((6,)), pltpu.SemaphoreType.DMA((2,))]
    scratch += [pltpu.SemaphoreType.DMA((len(scatter_plan), 2))]
    return pl.pallas_call(
        functools.partial(
            layer_kernel, grid, (pairs, length, width, hidden), (gather_plan, scatter_plan)
        ),
        out_shape=outs,
        in_specs=[pl.BlockSpec(memory_space=pltpu.SMEM)] + [vmem] * 9 + [hbm] * 5,
        out_specs=[hbm] * 7,
        scratch_shapes=scratch,
        compiler_params=pltpu.CompilerParams(
            collective_id=0, has_side_effects=True, vmem_limit_bytes=63 * 1024 * 1024
        ),
        name="encoder_layer",
    )(counts, *small, inputs, cotangent, triple, project, expand, shrink)


def shards(
    inputs,
    patch_count,
    cotangent,
    first_gain,
    first_shift,
    triple_weight,
    head_bias,
    output_weight,
    output_bias,
    second_gain,
    second_shift,
    expand_weight,
    expand_bias,
    reduce_weight,
    reduce_bias,
):
    fsdp, dp = lax.axis_size("fsdp"), lax.axis_size("dp")
    small = (
        first_gain,
        first_shift,
        head_bias,
        output_bias,
        second_gain,
        second_shift,
        expand_bias,
        reduce_bias,
    )
    layer_output, input_gradient, *shares, small_sums = run_layer(
        fsdp,
        dp,
        patch_count,
        [item.reshape(1, -1) for item in small],
        inputs,
        cotangent,
        triple_weight,
        output_weight,
        expand_weight,
        reduce_weight,
    )
    shrink_sum, expand_sum, project_sum, triple_sum = (item.astype(WIDE) for item in shares)
    (
        gain_one_sum,
        shift_one_sum,
        head_bias_sum,
        project_bias_sum,
        gain_two_sum,
        shift_two_sum,
        expand_add_sum,
        shrink_add_sum,
    ) = (small_sums[index, : item.shape[0]].astype(WIDE) for index, item in enumerate(small))
    return (
        layer_output,
        input_gradient,
        gain_one_sum,
        shift_one_sum,
        triple_sum,
        head_bias_sum,
        project_sum,
        project_bias_sum,
        gain_two_sum,
        shift_two_sum,
        expand_sum,
        expand_add_sum,
        shrink_sum,
        shrink_add_sum,
    )


def solution(mesh):
    in_specs = (
        P(("dp", "fsdp"), None, None),
        P(("dp", "fsdp")),
        P(("dp", "fsdp"), None, None),
        P("fsdp"),
        P("fsdp"),
        P("fsdp", None),
        P("fsdp"),
        P("fsdp", None),
        P("fsdp"),
        P("fsdp"),
        P("fsdp"),
        P("fsdp", None),
        P("fsdp"),
        P("fsdp", None),
        P("fsdp"),
    )
    out_specs = (
        P(("dp", "fsdp"), None, None),
        P(("dp", "fsdp"), None, None),
        P("fsdp"),
        P("fsdp"),
        P("fsdp", None),
        P("fsdp"),
        P("fsdp", None),
        P("fsdp"),
        P("fsdp"),
        P("fsdp"),
        P("fsdp", None),
        P("fsdp"),
        P("fsdp", None),
        P("fsdp"),
    )
    return jax.shard_map(shards, mesh=mesh, in_specs=in_specs, out_specs=out_specs, check_vma=False)
```
